256 devices in a mesh: ia: 8 (over y, core), ja: 8 (over z), ka: 4 (over x).
Axes of the slice: x: 4, y: 4, z: 8, core: 2. Of those that a mesh axis runs over, the one named last changes fastest.
Arguments:
- blocks: bfloat16 [256, 64, 64, 128], P(('ia', 'ja', 'ka')), may hold values from -6 to 6
- coords: int32 [3, 256], P(None, ('ia', 'ja', 'ka')), may hold values from 0 to 31, as said below
- live: int32 [256], P(('ia', 'ja', 'ka')), may hold values from 1 to 1, as said below
- factor_b: float32 [2048, 128], P('ja'), may hold values from -0.9 to 12
- factor_c: float32 [2048, 128], P('ka'), may hold values from -0.9 to 12
Outputs:
- loading_a: float32 [2048, 128], P('ia')
- loading_b: float32 [2048, 128], P('ja')
- loading_c: float32 [2048, 128], P('ka')
The draws below stay inside these ranges and needn't reach their ends.
Inputs may be any that keep to these rules, and one draw needn't show every extreme that they name: `live`: slot d holds the block of device d (devices counted along ia, ja, ka, ia slowest). The slots of device (p, q, s) name blocks with coords[0] from p * 4 to p * 4 + 3, coords[1] from q * 4 to q * 4 + 3, coords[2] from s * 4 to s * 4 + 3; each device's slot names one block of its own 4 x 4 x 4 block region.
All inputs are finite; a program needn't handle non-finite values.
Results may differ from the reference program's by a relative error of at most 0.0057.
Values sent between devices are 32-bit elements; how exact they have to be, the bound alone decides.
No kernel may reach another device: no remote copies, remote signals or barrier semaphores. Data moves between devices by JAX's collectives and lax.ppermute only.
A program may use at most 64 MiB of HBM per device.

```python
import jax
import jax.numpy as jnp
from jax import lax

RANK = 128
BI = 64
BJ = 64
BK = 128
GI_DEV = 4
GJ_DEV = 4
GK_DEV = 4
SLOTS = 1
ROWS_I = 2048
ROWS_J = 2048
ROWS_K = 2048
ALL_SLOTS = 256
N_IA = 8
N_JA = 8
N_KA = 4


def draw_coords(key, part):
    devices_all = N_IA * N_JA * N_KA
    cell_count = GI_DEV * GJ_DEV * GK_DEV
    key_list = jax.random.split(key, devices_all)
    chosen = jax.vmap(lambda single: jax.random.permutation(single, cell_count)[:SLOTS])(key_list)
    device = jnp.arange(devices_all, dtype=jnp.int32)[:, None]
    plane_i = device // (N_JA * N_KA)
    plane_j = device // N_KA % N_JA
    plane_k = device % N_KA
    local_i = chosen // (GJ_DEV * GK_DEV)
    local_j = chosen // GK_DEV % GJ_DEV
    local_k = chosen % GK_DEV
    stacked = jnp.stack([(plane_i * GI_DEV + local_i).reshape(-1), (plane_j * GJ_DEV + local_j).reshape(-1), (plane_k * GK_DEV + local_k).reshape(-1)])
    return stacked.astype(jnp.int32)


def draw_live(key, part):
    devices_all = N_IA * N_JA * N_KA
    drawn = jax.random.randint(key, (devices_all,), 0, SLOTS)
    counts = 1 + drawn * drawn // max(SLOTS - 1, 1)
    busiest = jax.random.randint(jax.random.fold_in(key, 11), (), 0, devices_all)
    return counts.at[busiest].set(SLOTS).astype(jnp.int32)


def factor_rows(key, count_rows):
    return 0.6 + 0.3 * jax.random.truncated_normal(key, -3.0, 3.0, (count_rows, RANK), jnp.float32)


def draw_factor_b(key, part):
    return factor_rows(key, ROWS_J)


def draw_factor_c(key, part):
    return factor_rows(key, ROWS_K)


def shard_levels(key, shape, cuts, least, top_value):
    def one(position, shards_of):
        draws = jax.random.uniform(jax.random.fold_in(jax.random.fold_in(key, 6), position), (shards_of,), jnp.float32, least / len(cuts), top_value / len(cuts))
        return jnp.repeat(jnp.exp(draws), shape[position] // shards_of).reshape((-1,) + (1,) * (len(shape) - position - 1))

    loudness = one(*cuts[0])
    for cut in cuts[1:]:
        loudness = loudness * one(*cut)
    return loudness


def centred(key, shape, spread, limit, pieces=(), kind=jnp.bfloat16):
    array = spread * jax.random.normal(key, shape, jnp.float32)
    if pieces:
        array = array * shard_levels(key, shape, pieces, -0.22, 0.18)
    return jnp.clip(array, -limit, limit).astype(kind)


def setup_inputs(seed: int = 0) -> dict:
    streams_of = jax.random.split(jax.random.key(seed), 6)
    return {
        "blocks": centred(streams_of[0], (ALL_SLOTS, BI, BJ, BK), 1.0, 6.0, ((0, 256),)),
        "coords": draw_coords(jax.random.fold_in(streams_of[5], 71), 0),
        "live": draw_live(jax.random.fold_in(streams_of[5], 71), 0),
        "factor_b": draw_factor_b(jax.random.fold_in(streams_of[5], 71), 0),
        "factor_c": draw_factor_c(jax.random.fold_in(streams_of[5], 71), 0),
    }


RIDGE_SHARE = 0.3
EPSILON = 1e-06
HIGHEST = lax.Precision.HIGHEST
sweep_order = (0, 1, 2)

def mean_gram(factor):
    return jnp.dot(factor.T.astype(jnp.float32), factor.astype(jnp.float32), precision=HIGHEST, preferred_element_type=jnp.float32) / factor.shape[0]

def factorize(gram_one, gram_two):
    merged = gram_one * gram_two
    order_rank = merged.shape[0]
    shift_value = RIDGE_SHARE * jnp.trace(merged) / order_rank
    lower_factor = jnp.linalg.cholesky(merged + shift_value * jnp.eye(order_rank, dtype=jnp.float32))
    return lax.linalg.triangular_solve(lower_factor, jnp.eye(order_rank, dtype=jnp.float32), left_side=True, lower=True)

def apply_inverse(inverse_lower, values):
    middle = jnp.dot(values.astype(jnp.float32), inverse_lower.T.astype(jnp.float32), precision=HIGHEST, preferred_element_type=jnp.float32)
    return jnp.dot(middle.astype(jnp.float32), inverse_lower.astype(jnp.float32), precision=HIGHEST, preferred_element_type=jnp.float32)

def normalize(solved):
    squares = lax.optimization_barrier(jnp.sum(solved * solved, axis=0)) / solved.shape[0]
    scaled = solved * lax.rsqrt(squares + EPSILON)
    return (scaled, mean_gram(scaled))

def block_product(mode_now, tensor_block, rows_one, rows_two):
    khatri = (rows_one[:, None, :] * rows_two[None, :, :]).astype(jnp.bfloat16)
    kept_dims = tuple((axis_id for axis_id in range(3) if axis_id != mode_now))
    return lax.dot_general(tensor_block.astype(jnp.float32), khatri.astype(jnp.float32), ((kept_dims, (0, 1)), ((), ())), precision=HIGHEST, preferred_element_type=jnp.float32)

def mttkrp(mode_now, blocks, coords, live, factors, length_rows):
    extents = (BI, BJ, BK)
    others = tuple((axis_id for axis_id in range(3) if axis_id != mode_now))
    slot_ids = jnp.arange(blocks.shape[0], dtype=jnp.int32)
    active = slot_ids % SLOTS < jnp.repeat(live, SLOTS)

    def visit(summed, slot_index):

        def accumulate(carried):
            tensor_block = lax.dynamic_index_in_dim(blocks, slot_index, 0, keepdims=False)
            rows_one = lax.dynamic_slice_in_dim(factors[others[0]], (coords[others[0], slot_index] * extents[others[0]]).astype(jnp.int32), extents[others[0]], 0)
            rows_two = lax.dynamic_slice_in_dim(factors[others[1]], (coords[others[1], slot_index] * extents[others[1]]).astype(jnp.int32), extents[others[1]], 0)
            product_rows = block_product(mode_now, tensor_block, rows_one, rows_two)
            offset = (coords[mode_now, slot_index] * extents[mode_now]).astype(jnp.int32)
            current = lax.dynamic_slice_in_dim(carried, offset, extents[mode_now], 0)
            return lax.dynamic_update_slice_in_dim(carried, current + product_rows, offset, 0)

        def unchanged(carried):
            return carried
        return (lax.cond(active[slot_index], accumulate, unchanged, summed), None)
    start_rows = jnp.zeros((length_rows, RANK), jnp.float32)
    return lax.scan(visit, start_rows, slot_ids)[0]

def reference(blocks, coords, live, factor_b, factor_c):
    lengths = (ROWS_I, ROWS_J, ROWS_K)
    factors = [jnp.zeros((ROWS_I, RANK), jnp.float32), factor_b, factor_c]
    gram_list = [None, mean_gram(factor_b), mean_gram(factor_c)]
    for mode_now in sweep_order:
        others = tuple((axis_id for axis_id in range(3) if axis_id != mode_now))
        summed = mttkrp(mode_now, blocks, coords, live, factors, lengths[mode_now])
        inverse_lower = factorize(gram_list[others[0]], gram_list[others[1]])
        factors[mode_now], gram_list[mode_now] = normalize(apply_inverse(inverse_lower, summed))
    return (factors[0], factors[1], factors[2])
```

```python
import jax
import jax.numpy as jnp
from jax import lax
from jax.sharding import PartitionSpec as P

RANK = 128
BI = 64
BJ = 64
BK = 128
GI_DEV = 4
GJ_DEV = 4
GK_DEV = 4
SLOTS = 4

RIDGE_SHARE = 0.3
EPSILON = 1e-06
HIGHEST = lax.Precision.HIGHEST


def factorize(merged):
    order_rank = merged.shape[0]
    shift_value = RIDGE_SHARE * jnp.trace(merged) / order_rank
    lower_factor = jnp.linalg.cholesky(
        merged + shift_value * jnp.eye(order_rank, dtype=jnp.float32)
    )
    return lax.linalg.triangular_solve(
        lower_factor, jnp.eye(order_rank, dtype=jnp.float32), left_side=True, lower=True
    )


def exact_dot(left, right):
    return jnp.dot(left, right, precision=HIGHEST, preferred_element_type=jnp.float32)


def apply_inverse(inverse_lower, values):
    return exact_dot(exact_dot(values, inverse_lower.T), inverse_lower)


def gram(rows):
    return exact_dot(rows.T, rows)


def block_product(mode_now, tensor_block, rows_one, rows_two, split):
    product = rows_one[:, None, :] * rows_two[None, :, :]
    kept = tuple(axis_id for axis_id in range(3) if axis_id != mode_now)
    dims = ((kept, (0, 1)), ((), ()))
    high = product.astype(jnp.bfloat16)
    total = lax.dot_general(tensor_block, high, dims, preferred_element_type=jnp.float32)
    if split:
        low = (product - high.astype(jnp.float32)).astype(jnp.bfloat16)
        total = total + lax.dot_general(
            tensor_block, low, dims, preferred_element_type=jnp.float32
        )
    return total


def exchange(values, axes):
    return lax.all_to_all(values, axes, 0, 0, tiled=True)


def scatter_sum(parts, slot_ids):
    rows = []
    for slot in range(SLOTS):
        picked = jnp.where((slot_ids == slot)[:, None, None], parts, 0.0)
        rows.append(jnp.sum(picked, axis=0))
    return jnp.concatenate(rows, axis=0)


def reduce_rows(axes, count, partial, slot, extras):
    pieces = [partial.reshape(count, 2, RANK)]
    pieces += [extra.reshape(count, -1, RANK) for extra in extras]
    pieces.append(jnp.full((count, 1, RANK), slot.astype(jnp.float32)))
    used = sum(piece.shape[1] for piece in pieces)
    if used % 8:
        pieces.append(jnp.zeros((count, 8 - used % 8, RANK), jnp.float32))
    got = exchange(jnp.concatenate(pieces, axis=1), axes)
    slot_ids = got[:, used - 1, 0].astype(jnp.int32)
    own = scatter_sum(got[:, 0:2], slot_ids)
    sums = jnp.sum(got[:, 2 : used - 1], axis=0)
    return own, sums


def spread_rows(axes, count, own):
    return exchange(jnp.broadcast_to(own[None], (count,) + own.shape), axes)


def in_order(rows):
    count = rows.shape[0]
    return rows.reshape(count, SLOTS, 2, RANK).transpose(1, 0, 2, 3).reshape(-1, RANK)


def slot_rows(rows, slot):
    count = rows.shape[0]
    return lax.dynamic_slice_in_dim(rows, slot * 2, 2, 1).reshape(count * 2, RANK)


def on_device(blocks, coords, live, factor_b, factor_c):
    at_i, at_j, at_k = (lax.axis_index(name) for name in ("ia", "ja", "ka"))
    slot_i = coords[0, 0] - at_i * GI_DEV
    slot_j = coords[1, 0] - at_j * GJ_DEV
    slot_k = coords[2, 0] - at_k * GK_DEV
    block = blocks[0]
    eye = jnp.eye(RANK, dtype=jnp.float32)
    upper = jnp.triu(jnp.ones((RANK, RANK), jnp.bool_))

    rows_b = lax.dynamic_slice_in_dim(factor_b, slot_j * BJ, BJ, 0)
    rows_c = lax.dynamic_slice_in_dim(factor_c, slot_k * BK, BK, 0)
    partial = block_product(0, block, rows_b, rows_c, False)
    part_b = gram(lax.dynamic_slice_in_dim(factor_b, at_k * 64, 64, 0)) / 2048
    part_c = gram(lax.dynamic_slice_in_dim(factor_c, at_j * 64, 64, 0)) / 2048
    packed = jnp.where(upper, part_b, part_c)
    diagonal = jnp.sum(part_c * eye, axis=0)
    own, sums = reduce_rows(
        ("ja", "ka"), 32, partial, slot_i, [packed, jnp.tile(diagonal[None], (32, 1))]
    )
    got = spread_rows(("ja", "ka"), 32, jnp.concatenate([own, sums[0:4]], axis=0))
    packed = got[:, 8:12].reshape(RANK, RANK)
    strict = jnp.logical_and(upper, eye == 0.0)
    gram_b = jnp.where(upper, packed, packed.T)
    gram_c = jnp.where(strict, packed.T, jnp.where(upper, sums[4][None, :] * eye, packed))
    inverse_lower = factorize(gram_b * gram_c)
    solved_a = apply_inverse(inverse_lower, got[:, 0:8].reshape(256, RANK)).reshape(32, 8, RANK)
    own_a = slot_rows(solved_a, slot_i)

    partial = block_product(1, block, own_a, rows_c, True)
    share = lax.dynamic_slice_in_dim(solved_a, at_k * 8, 8, 0).reshape(64, RANK)
    own, sums = reduce_rows(("ia", "ka"), 32, partial, slot_j, [gram(share)])
    got = spread_rows(("ia", "ka"), 32, jnp.concatenate([own, sums], axis=0))
    raw = got[:, 8:12].reshape(RANK, RANK) / 2048
    scale_a = lax.rsqrt(jnp.sum(raw * eye, axis=0) + EPSILON)
    gram_a = raw * scale_a[:, None] * scale_a[None, :]
    inverse_lower = factorize(gram_a * gram_c)
    solved_b = apply_inverse(
        inverse_lower, got[:, 0:8].reshape(256, RANK) * scale_a
    ).reshape(32, 8, RANK)
    own_b = slot_rows(solved_b, slot_j)

    partial = block_product(2, block, own_a * scale_a, own_b, True)
    share = lax.dynamic_slice_in_dim(solved_b, at_i * 4, 4, 0).reshape(32, RANK)
    own, sums = reduce_rows(("ia", "ja"), 64, partial, slot_k, [gram(share)])
    got = spread_rows(("ia", "ja"), 64, jnp.concatenate([own, sums], axis=0))
    raw = got[:, 8:10].reshape(RANK, RANK) / 2048
    scale_b = lax.rsqrt(jnp.sum(raw * eye, axis=0) + EPSILON)
    gram_b = raw * scale_b[:, None] * scale_b[None, :]
    inverse_lower = factorize(gram_a * gram_b)
    solved_c = apply_inverse(inverse_lower, got[:, 0:8].reshape(512, RANK) * scale_b)
    squares = jnp.sum(solved_c * solved_c, axis=0, keepdims=True)
    total = squares
    for step in (1, 2, 3):
        total = total + lax.ppermute(squares, "ka", [(n, (n + step) % 4) for n in range(4)])
    scale_c = lax.rsqrt(total / 2048 + EPSILON)

    loading_a = in_order(solved_a * scale_a)
    loading_b = in_order(solved_b * scale_b)
    loading_c = in_order((solved_c * scale_c).reshape(64, 8, RANK))
    return (loading_a, loading_b, loading_c)


def solution(mesh):
    placed = (
        P(("ia", "ja", "ka"), None, None, None),
        P(None, ("ia", "ja", "ka")),
        P(("ia", "ja", "ka")),
        P("ja", None),
        P("ka", None),
    )
    return jax.shard_map(
        on_device,
        mesh=mesh,
        in_specs=placed,
        out_specs=(P("ia", None), P("ja", None), P("ka", None)),
        check_vma=False,
    )
```

```python
import functools

import jax
import jax.numpy as jnp
from jax import lax
from jax.experimental import pallas as pl
from jax.experimental.pallas import tpu as pltpu
from jax.sharding import PartitionSpec as P

RANK = 128
BI = 64
BJ = 64
BK = 128
GI_DEV = 4
GJ_DEV = 4
GK_DEV = 4
SLOTS = 4
ROWS = 2048

RIDGE_SHARE = 0.3
EPSILON = 1e-06
HIGHEST = lax.Precision.HIGHEST
F32 = jnp.float32
BF16 = jnp.bfloat16


def exact_dot(left, right):
    return jnp.dot(left, right, precision=HIGHEST, preferred_element_type=F32)


def gram(rows):
    return lax.dot_general(
        rows, rows, (((0,), (0,)), ((), ())), precision=HIGHEST, preferred_element_type=F32
    )


def halves(values):
    high = values.astype(BF16)
    return high, (values - high.astype(F32)).astype(BF16)


def iotas():
    shape = (RANK, RANK)
    return lax.broadcasted_iota(jnp.int32, shape, 0), lax.broadcasted_iota(jnp.int32, shape, 1)


def inverse(matrix):
    count = RANK // 8
    rows = [matrix[8 * n : 8 * n + 8, :] for n in range(count)]
    lane = lax.broadcasted_iota(jnp.int32, (8, RANK), 1)
    sub = lax.broadcasted_iota(jnp.int32, (8, RANK), 0)

    def over_lanes(tile, at):
        return jnp.broadcast_to(tile[:, at : at + 1], (8, RANK))

    def over_rows(tile, at):
        return jnp.broadcast_to(tile[at : at + 1, :], (8, RANK))

    for k in range(count):
        panel = rows[k]
        columns = [over_lanes(panel, 8 * k + t) for t in range(8)]
        inside = (lane >= 8 * k) & (lane < 8 * k + 8)
        panel = jnp.where(inside, jnp.where(lane - 8 * k == sub, 1.0, 0.0), panel)
        for s in range(8):
            pivot = 1.0 / over_rows(columns[s], s)
            factor = columns[s]
            lead = over_rows(panel, s) * pivot
            panel = jnp.where(sub == s, lead, panel - factor * lead)
            for t in range(s + 1, 8):
                lead = over_rows(columns[t], s) * pivot
                columns[t] = jnp.where(sub == s, lead, columns[t] - factor * lead)
        leads = [over_rows(panel, s) for s in range(8)]
        for step in range(count - 1):
            n = (k + 1 + step) % count
            terms = [over_lanes(rows[n], 8 * k + s) * leads[s] for s in range(8)]
            while len(terms) > 1:
                terms = [terms[i] + terms[i + 1] for i in range(0, len(terms), 2)]
            rows[n] = jnp.where(inside, 0.0, rows[n]) - terms[0]
        rows[k] = panel
    return jnp.concatenate(rows, axis=0)


def system_inverse(merged):
    row, col = iotas()
    shift = jnp.sum(jnp.where(row == col, merged, 0.0)) * (RIDGE_SHARE / RANK)
    return inverse(merged + jnp.where(row == col, shift, 0.0))


def strided(ref, start, count, step):
    return ref[pl.ds(start, count, stride=step), :]


def put(ref, start, count, step, value):
    ref[pl.ds(start, count, stride=step), :] = value


def scaled_gram(raw):
    row, col = iotas()
    diagonal = jnp.where(row == col, raw, 0.0)
    across = lax.rsqrt(jnp.sum(diagonal, axis=0, keepdims=True) + EPSILON)
    down = lax.rsqrt(jnp.sum(diagonal, axis=1, keepdims=True) + EPSILON)
    return across, raw * down * across


def places(coords_ref):
    at = [lax.axis_index(name) for name in ("ia", "ja", "ka")]
    return at, [coords_ref[n, 0] - 4 * at[n] for n in range(3)]


def some_rows(ref, index, size):
    return ref[pl.ds(pl.multiple_of(index * size, size), size), :]


def first_kernel(coords_ref, block_ref, b_ref, c_ref, chunk_ref, y_ref):
    at, slot = places(coords_ref)
    high, low = halves(some_rows(c_ref, slot[2], BK))
    block = block_ref[...].reshape(BI * BJ, BK)
    y_ref[...] = jnp.dot(
        jnp.concatenate([block, block], axis=1),
        jnp.concatenate([high, low], axis=0),
        preferred_element_type=F32,
    ).reshape(BI, BJ, RANK)
    rows_b = some_rows(b_ref, slot[1], BJ)
    partial = jnp.concatenate(
        [jnp.sum(y_ref[n] * rows_b, axis=0, keepdims=True) for n in range(BI)], axis=0
    )
    part_b = gram(some_rows(b_ref, at[2], 64)) * (1.0 / ROWS)
    part_c = gram(some_rows(c_ref, at[1], 64)) * (1.0 / ROWS)
    row, col = iotas()
    packed = jnp.where(row <= col, part_b, part_c)
    diagonal = jnp.sum(jnp.where(row == col, part_c, 0.0), axis=0, keepdims=True)
    for t in range(2):
        put(chunk_ref, t, 32, 8, partial[32 * t : 32 * t + 32])
    for t in range(4):
        put(chunk_ref, 2 + t, 32, 8, packed[32 * t : 32 * t + 32])
    put(chunk_ref, 6, 32, 8, jnp.broadcast_to(diagonal, (32, RANK)))
    put(chunk_ref, 7, 32, 8, jnp.full((32, RANK), slot[0].astype(F32)))


def collect(got_ref, count, extras):
    ids = strided(got_ref, 7, count, 8)
    rows = []
    for slot in range(SLOTS):
        for t in range(2):
            picked = jnp.where(ids == slot, strided(got_ref, t, count, 8), 0.0)
            rows.append(jnp.sum(picked, axis=0, keepdims=True))
    for t in range(extras):
        rows.append(jnp.sum(strided(got_ref, 2 + t, count, 8), axis=0, keepdims=True))
    return rows


def repeat_rows(ref, rows, copies):
    width = len(rows)
    unit = 1
    while width * unit % 8:
        unit *= 2
    tile = jnp.concatenate(rows * unit, axis=0)
    for n in range(copies // unit):
        ref[n * width * unit : (n + 1) * width * unit, :] = tile


def collect_first_kernel(got_ref, spread_ref, diagonal_ref):
    rows = collect(got_ref, 32, 5)
    repeat_rows(spread_ref, rows[:12], 32)
    diagonal_ref[...] = jnp.broadcast_to(rows[12], (8, RANK))


def collect_kernel(count, extras, got_ref, spread_ref):
    repeat_rows(spread_ref, collect(got_ref, count, extras), count)


def natural(got_ref, count, step, first, last):
    return jnp.concatenate([strided(got_ref, t, count, step) for t in range(first, last)], axis=0)


def second_kernel(coords_ref, got_ref, diagonal_ref, y_ref, solved_ref, chunk_ref, gram_c_ref):
    at, slot = places(coords_ref)
    packed = natural(got_ref, 32, 12, 8, 12)
    flipped = packed.T
    row, col = iotas()
    gram_b = jnp.where(row <= col, packed, flipped)
    gram_c = jnp.where(row < col, flipped, packed)
    gram_c = jnp.where(row == col, diagonal_ref[0:1, :], gram_c)
    gram_c_ref[...] = gram_c
    solver = system_inverse(gram_b * gram_c)
    solved_ref[...] = exact_dot(natural(got_ref, 32, 12, 0, 8), solver)
    raw = gram(some_rows(solved_ref, at[2], 64)) * (1.0 / ROWS)
    own = some_rows(solved_ref, slot[0], BI)
    sums = [jnp.zeros((BJ, RANK), F32) for _ in range(2)]
    for n in range(BI):
        sums[n % 2] = sums[n % 2] + own[n : n + 1, :] * y_ref[n]
    partial = sums[0] + sums[1]
    for t in range(2):
        put(chunk_ref, t, 32, 8, partial[32 * t : 32 * t + 32])
    for t in range(4):
        put(chunk_ref, 2 + t, 32, 8, raw[32 * t : 32 * t + 32])
    put(chunk_ref, 6, 32, 8, jnp.zeros((32, RANK), F32))
    put(chunk_ref, 7, 32, 8, jnp.full((32, RANK), slot[1].astype(F32)))


def third_kernel(
    coords_ref, got_ref, gram_c_ref, solved_a_ref, block_ref,
    loading_a_ref, solved_ref, chunk_ref, gram_a_ref, khatri_ref,
):
    at, slot = places(coords_ref)
    scale, gram_a = scaled_gram(natural(got_ref, 32, 12, 8, 12))
    gram_a_ref[...] = gram_a
    loading_a_ref[...] = solved_a_ref[...] * scale
    solver = system_inverse(gram_a * gram_c_ref[...])
    solved_ref[...] = exact_dot(natural(got_ref, 32, 12, 0, 8) * scale, solver)
    raw = gram(some_rows(solved_ref, at[0], 32)) * (1.0 / ROWS)
    own_a = some_rows(loading_a_ref, slot[0], BI)
    own_b = some_rows(solved_ref, slot[1], BJ)
    for n in range(BI):
        khatri_ref[n * BJ : (n + 1) * BJ, :] = (own_a[n : n + 1, :] * own_b).astype(BF16)
    partial = lax.dot_general(
        block_ref[...].reshape(BI * BJ, BK),
        khatri_ref[...],
        (((0,), (0,)), ((), ())),
        preferred_element_type=F32,
    )
    for t in range(2):
        put(chunk_ref, t, 64, 8, partial[64 * t : 64 * t + 64])
    for t in range(2):
        put(chunk_ref, 2 + t, 64, 8, raw[64 * t : 64 * t + 64])
    for t in range(4, 7):
        put(chunk_ref, t, 64, 8, jnp.zeros((64, RANK), F32))
    put(chunk_ref, 7, 64, 8, jnp.full((64, RANK), slot[2].astype(F32)))


def fourth_kernel(got_ref, gram_a_ref, solved_b_ref, loading_b_ref, solved_ref, squares_ref):
    scale, gram_b = scaled_gram(natural(got_ref, 64, 10, 8, 10))
    loading_b_ref[...] = solved_b_ref[...] * scale
    solver = system_inverse(gram_a_ref[...] * gram_b)
    solved = exact_dot(natural(got_ref, 64, 10, 0, 8) * scale, solver)
    solved_ref[...] = solved
    squares_ref[...] = jnp.sum(solved * solved, axis=0, keepdims=True)


def call(kernel, operands, outs, name, scalars=0, scratch=()):
    vmem = pl.BlockSpec(memory_space=pltpu.VMEM)
    smem = pl.BlockSpec(memory_space=pltpu.SMEM)
    return pl.pallas_call(
        kernel,
        out_shape=[jax.ShapeDtypeStruct(shape, F32) for shape in outs],
        in_specs=[smem] * scalars + [vmem] * (len(operands) - scalars),
        out_specs=[vmem] * len(outs),
        scratch_shapes=scratch,
        compiler_params=pltpu.CompilerParams(vmem_limit_bytes=32 << 20),
        name=name,
    )(*operands)


def exchange(values, axes, *chunk):
    shape = values.shape
    return lax.all_to_all(values.reshape(chunk), axes, 0, 0, tiled=True).reshape(shape)


def on_device(blocks, coords, live, factor_b, factor_c):
    block = blocks[0]
    full = (RANK, RANK)

    chunk, y = call(
        first_kernel, (coords, block, factor_b, factor_c), [(256, RANK), (BI, BJ, RANK)], "first", 1
    )
    got = exchange(chunk, ("ja", "ka"), 32, 8, RANK)
    spread, diagonal = call(collect_first_kernel, (got,), [(384, RANK), (8, RANK)], "collect_a")
    got = exchange(spread, ("ja", "ka"), 32, 3, 4, RANK)

    solved_a, chunk, gram_c = call(
        second_kernel, (coords, got, diagonal, y), [(256, RANK), (256, RANK), full], "second", 1
    )
    got = exchange(chunk, ("ia", "ka"), 32, 8, RANK)
    (spread,) = call(functools.partial(collect_kernel, 32, 4), (got,), [(384, RANK)], "collect_b")
    got = exchange(spread, ("ia", "ka"), 32, 3, 4, RANK)

    loading_a, solved_b, chunk, gram_a = call(
        third_kernel,
        (coords, got, gram_c, solved_a, block),
        [(256, RANK), (256, RANK), (512, RANK), full],
        "third",
        1,
        [pltpu.VMEM((BI * BJ, RANK), BF16)],
    )
    got = exchange(chunk, ("ia", "ja"), 64, 8, RANK)
    (spread,) = call(functools.partial(collect_kernel, 64, 2), (got,), [(640, RANK)], "collect_c")
    got = exchange(spread, ("ia", "ja"), 64, 5, 2, RANK)

    loading_b, solved_c, squares = call(
        fourth_kernel, (got, gram_a, solved_b), [(256, RANK), (512, RANK), (1, RANK)], "fourth"
    )
    total = squares
    for step in (1, 2, 3):
        total = total + lax.ppermute(squares, "ka", [(n, (n + step) % 4) for n in range(4)])
    loading_c = solved_c * lax.rsqrt(total / ROWS + EPSILON)
    return (loading_a, loading_b, loading_c)


def solution(mesh):
    placed = (
        P(("ia", "ja", "ka"), None, None, None),
        P(None, ("ia", "ja", "ka")),
        P(("ia", "ja", "ka")),
        P("ja", None),
        P("ka", None),
    )
    return jax.shard_map(
        on_device,
        mesh=mesh,
        in_specs=placed,
        out_specs=(P("ia", None), P("ja", None), P("ka", None)),
        check_vma=False,
    )
```

```python
import jax
import jax.numpy as jnp
from jax import lax
from jax.experimental import pallas as pl
from jax.experimental.pallas import tpu as pltpu
from jax.sharding import PartitionSpec as P

RANK = 128
BI = 64
BJ = 64
BK = 128
GI_DEV = 4
GJ_DEV = 4
GK_DEV = 4
SLOTS = 4
ROWS = 2048
IA = ("iy", "ic")

RIDGE_SHARE = 0.3
EPSILON = 1e-06
HIGHEST = lax.Precision.HIGHEST
F32 = jnp.float32
BF16 = jnp.bfloat16


def exact_dot(left, right):
    return jnp.dot(left, right, precision=HIGHEST, preferred_element_type=F32)


def gram(rows):
    return lax.dot_general(
        rows, rows, (((0,), (0,)), ((), ())), precision=HIGHEST, preferred_element_type=F32
    )


def halves(values):
    high = values.astype(BF16)
    return high, (values - high.astype(F32)).astype(BF16)


def iotas():
    shape = (RANK, RANK)
    return lax.broadcasted_iota(jnp.int32, shape, 0), lax.broadcasted_iota(jnp.int32, shape, 1)


def inverse(matrix):
    count = RANK // 8
    rows = [matrix[8 * n : 8 * n + 8, :] for n in range(count)]
    lane = lax.broadcasted_iota(jnp.int32, (8, RANK), 1)
    sub = lax.broadcasted_iota(jnp.int32, (8, RANK), 0)

    def over_lanes(tile, at):
        return jnp.broadcast_to(tile[:, at : at + 1], (8, RANK))

    def over_rows(tile, at):
        return jnp.broadcast_to(tile[at : at + 1, :], (8, RANK))

    one = jnp.clip(rows[0], 1.0, 1.0)
    for k in range(count):
        panel = rows[k]
        columns = [over_lanes(panel, 8 * k + t) * one for t in range(8)]
        inside = (lane >= 8 * k) & (lane < 8 * k + 8)
        panel = jnp.where(inside, jnp.where(lane - 8 * k == sub, 1.0, 0.0), panel)
        for s in range(8):
            pivot = over_rows(1.0 / columns[s], s)
            factor = jnp.where(sub == s, 0.0, columns[s]) * pivot
            keep = jnp.where(sub == s, pivot, 1.0)
            panel = panel * keep - factor * over_rows(panel, s)
            for t in range(s + 1, 8):
                columns[t] = columns[t] * keep - factor * over_rows(columns[t], s)
        leads = [over_rows(panel, s) for s in range(8)]
        for step in range(count - 1):
            n = (k + 1 + step) % count
            terms = [over_lanes(rows[n], 8 * k + s) * leads[s] for s in range(8)]
            while len(terms) > 1:
                terms = [terms[i] + terms[i + 1] for i in range(0, len(terms), 2)]
            rows[n] = jnp.where(inside, 0.0, rows[n]) - terms[0]
        rows[k] = panel
    return jnp.concatenate(rows, axis=0)


def system_inverse(merged):
    row, col = iotas()
    shift = jnp.sum(jnp.where(row == col, merged, 0.0)) * (RIDGE_SHARE / RANK)
    return inverse(merged + jnp.where(row == col, shift, 0.0))


def strided(ref, start, count, step):
    return ref[pl.ds(start, count, stride=step), :]


def put(ref, start, count, step, value):
    ref[pl.ds(start, count, stride=step), :] = value


def scaled_gram(raw):
    row, col = iotas()
    diagonal = jnp.where(row == col, raw, 0.0)
    across = lax.rsqrt(jnp.sum(diagonal, axis=0, keepdims=True) + EPSILON)
    down = lax.rsqrt(jnp.sum(diagonal, axis=1, keepdims=True) + EPSILON)
    return across, raw * down * across


def places(coords_ref):
    at = [lax.axis_index(IA), lax.axis_index("ja"), lax.axis_index("ka")]
    return at, [coords_ref[n] - 4 * at[n] for n in range(3)]


def some_rows(ref, index, size):
    return ref[pl.ds(pl.multiple_of(index * size, size), size), :]


def first_kernel(
    coords_ref, block_ref, b_ref, c_ref, chunk_ref, y_ref,
    x_in, c_in, b_in, share_c, share_b, sems,
):
    at, slot = places(coords_ref)

    def window(ref, index, size):
        return ref.at[pl.ds(pl.multiple_of(index * size, size), size), :]

    small = [
        (window(c_ref, slot[2], BK), c_in),
        (window(b_ref, slot[1], BJ), b_in),
        (window(c_ref, at[1], 64), share_c),
        (window(b_ref, at[2], 64), share_b),
    ]
    parts = [pl.ds(n * (BI // 4), BI // 4) for n in range(4)]
    copies = [pltpu.make_async_copy(src, dst, sems.at[n]) for n, (src, dst) in enumerate(small)]
    copies += [
        pltpu.make_async_copy(block_ref.at[part], x_in.at[part], sems.at[4 + n])
        for n, part in enumerate(parts)
    ]
    for copy in copies:
        copy.start()
    for copy in copies[:4]:
        copy.wait()
    part_c = gram(share_c[...]) * (1.0 / ROWS)
    part_b = gram(share_b[...]) * (1.0 / ROWS)
    row, col = iotas()
    packed = jnp.where(row <= col, part_b, part_c)
    diagonal = jnp.sum(jnp.where(row == col, part_c, 0.0), axis=0, keepdims=True)
    for t in range(4):
        put(chunk_ref, 2 + t, 32, 8, packed[32 * t : 32 * t + 32])
    put(chunk_ref, 6, 32, 8, jnp.broadcast_to(diagonal, (32, RANK)))
    put(chunk_ref, 7, 32, 8, jnp.full((32, RANK), slot[0].astype(F32)))
    high, low = halves(c_in[...])
    both = jnp.concatenate([high, low], axis=0)
    rows_b = b_in[...]
    partial = []
    for n, part in enumerate(parts):
        copies[4 + n].wait()
        block = x_in[part].reshape(BI // 4 * BJ, BK)
        y = jnp.dot(jnp.concatenate([block, block], axis=1), both, preferred_element_type=F32)
        y = y.reshape(BI // 4, BJ, RANK)
        y_ref[part] = y
        partial += [jnp.sum(y[m] * rows_b, axis=0, keepdims=True) for m in range(BI // 4)]
    for t in range(2):
        put(chunk_ref, t, 32, 8, jnp.concatenate(partial[32 * t : 32 * t + 32], axis=0))


def collect(got_ref, count, step, ids, extras):
    rows = []
    for slot in range(SLOTS):
        for t in range(2):
            picked = jnp.where(ids == slot, strided(got_ref, t, count, step), 0.0)
            rows.append(jnp.sum(picked, axis=0, keepdims=True))
    for t in range(extras):
        rows.append(jnp.sum(strided(got_ref, 2 + t, count, step), axis=0, keepdims=True))
    return rows


def lower_lanes(values):
    lane = lax.broadcasted_iota(jnp.int32, values.shape, 1)
    return jnp.where(lane < 64, values, pltpu.roll(values, 64, 1))


def mark(rows, slot):
    lane = lax.broadcasted_iota(jnp.int32, rows.shape, 1)
    return jnp.where(lane < 64, slot.astype(F32), rows)


def unmark(raw):
    row, col = iotas()
    return jnp.where((row >= 64) & (col < 64), raw.T, raw)


def repeat_rows(ref, rows, copies):
    width = len(rows)
    unit = 1
    while width * unit % 8:
        unit *= 2
    tile = jnp.concatenate(rows * unit, axis=0)
    for n in range(copies // unit):
        ref[n * width * unit : (n + 1) * width * unit, :] = tile


def collect_first_kernel(got_ref, spread_ref, diagonal_ref):
    rows = collect(got_ref, 32, 8, strided(got_ref, 7, 32, 8), 5)
    repeat_rows(spread_ref, rows[:12], 32)
    diagonal_ref[...] = jnp.broadcast_to(rows[12], (8, RANK))


def collect_second_kernel(got_ref, spread_ref):
    rows = collect(got_ref, 32, 6, lower_lanes(strided(got_ref, 5, 32, 6)), 4)
    repeat_rows(spread_ref, rows, 32)


def collect_third_kernel(got_ref, spread_ref):
    rows = collect(got_ref, 64, 4, lower_lanes(strided(got_ref, 3, 64, 4)), 2)
    repeat_rows(spread_ref, rows, 32)


def natural(got_ref, count, step, first, last):
    return jnp.concatenate([strided(got_ref, t, count, step) for t in range(first, last)], axis=0)


def second_kernel(coords_ref, got_ref, diagonal_ref, y_ref, solved_ref, chunk_ref, gram_c_ref):
    at, slot = places(coords_ref)
    packed = natural(got_ref, 32, 12, 8, 12)
    flipped = packed.T
    row, col = iotas()
    gram_b = jnp.where(row <= col, packed, flipped)
    gram_c = jnp.where(row < col, flipped, packed)
    gram_c = jnp.where(row == col, diagonal_ref[0:1, :], gram_c)
    gram_c_ref[...] = gram_c
    solver = system_inverse(gram_b * gram_c)
    solved_ref[...] = exact_dot(natural(got_ref, 32, 12, 0, 8), solver)
    raw = gram(some_rows(solved_ref, at[2], 64)) * (1.0 / ROWS)
    own = some_rows(solved_ref, slot[0], BI)
    sums = [jnp.zeros((BJ, RANK), F32) for _ in range(2)]
    for n in range(BI):
        sums[n % 2] = sums[n % 2] + own[n : n + 1, :] * y_ref[n]
    partial = sums[0] + sums[1]
    for t in range(2):
        put(chunk_ref, t, 32, 6, partial[32 * t : 32 * t + 32])
    for t in range(4):
        rows = raw[32 * t : 32 * t + 32]
        put(chunk_ref, 2 + t, 32, 6, rows if t < 2 else mark(rows, slot[1]))


def third_kernel(
    coords_ref, got_ref, gram_c_ref, solved_a_ref, block_ref,
    loading_a_ref, solved_ref, chunk_ref, gram_a_ref, khatri_ref,
):
    at, slot = places(coords_ref)
    scale, gram_a = scaled_gram(unmark(natural(got_ref, 32, 12, 8, 12)))
    gram_a_ref[...] = gram_a
    loading_a_ref[...] = solved_a_ref[...] * scale
    solver = system_inverse(gram_a * gram_c_ref[...])
    solved_ref[...] = exact_dot(natural(got_ref, 32, 12, 0, 8) * scale, solver)
    raw = gram(some_rows(solved_ref, at[0], 32)) * (1.0 / ROWS)
    own_a = some_rows(loading_a_ref, slot[0], BI)
    own_b = some_rows(solved_ref, slot[1], BJ)
    for n in range(BI):
        khatri_ref[n * BJ : (n + 1) * BJ, :] = (own_a[n : n + 1, :] * own_b).astype(BF16)
    partial = lax.dot_general(
        block_ref[...].reshape(BI * BJ, BK),
        khatri_ref[...],
        (((0,), (0,)), ((), ())),
        preferred_element_type=F32,
    )
    for t in range(2):
        put(chunk_ref, t, 64, 4, partial[64 * t : 64 * t + 64])
    put(chunk_ref, 2, 64, 4, raw[0:64])
    put(chunk_ref, 3, 64, 4, mark(raw[64:128], slot[2]))


def fourth_kernel(
    same_ref, other_ref, gram_a_ref, solved_b_ref, loading_b_ref, solved_ref, squares_ref, rows_ref
):
    core = lax.axis_index("ic")
    for ref, half in ((same_ref, core), (other_ref, 1 - core)):
        for t in range(10):
            for n in range(4):
                place = pl.multiple_of(64 * t + 16 * n + 8 * half, 8)
                rows_ref[pl.ds(place, 8), :] = strided(ref, 80 * n + t, 8, 10)
    scale, gram_b = scaled_gram(unmark(rows_ref[512:640, :]))
    loading_b_ref[...] = solved_b_ref[...] * scale
    solver = system_inverse(gram_a_ref[...] * gram_b)
    solved = exact_dot(rows_ref[0:512, :] * scale, solver)
    solved_ref[...] = solved
    squares_ref[...] = jnp.sum(solved * solved, axis=0, keepdims=True)


def call(kernel, operands, outs, name, scalars=0, scratch=(), space=pltpu.VMEM):
    vmem = pl.BlockSpec(memory_space=pltpu.VMEM)
    smem = pl.BlockSpec(memory_space=pltpu.SMEM)
    return pl.pallas_call(
        kernel,
        out_shape=[jax.ShapeDtypeStruct(shape, F32) for shape in outs],
        in_specs=[smem] * scalars + [pl.BlockSpec(memory_space=space)] * (len(operands) - scalars),
        out_specs=[vmem] * len(outs),
        scratch_shapes=scratch,
        compiler_params=pltpu.CompilerParams(vmem_limit_bytes=32 << 20),
        name=name,
    )(*operands)


def exchange(values, axes, *chunk):
    shape = values.shape
    return lax.all_to_all(values.reshape(chunk), axes, 0, 0, tiled=True).reshape(shape)


def on_device(blocks, coords, live, factor_b, factor_c):
    block = blocks[0]
    coords = coords.reshape(3)
    full = (RANK, RANK)

    chunk, y = call(
        first_kernel,
        (coords, block, factor_b, factor_c),
        [(256, RANK), (BI, BJ, RANK)],
        "first",
        1,
        [
            pltpu.VMEM((BI, BJ, BK), BF16),
            pltpu.VMEM((BK, RANK), F32),
            pltpu.VMEM((BJ, RANK), F32),
            pltpu.VMEM((64, RANK), F32),
            pltpu.VMEM((64, RANK), F32),
            pltpu.SemaphoreType.DMA((8,)),
        ],
        pl.ANY,
    )
    got = exchange(chunk, ("ja", "ka"), 32, 8, RANK)
    spread, diagonal = call(collect_first_kernel, (got,), [(384, RANK), (8, RANK)], "collect_a")
    got = exchange(spread, ("ja", "ka"), 32, 3, 4, RANK)

    solved_a, chunk, gram_c = call(
        second_kernel, (coords, got, diagonal, y), [(256, RANK), (192, RANK), full], "second", 1
    )
    got = exchange(chunk, (*IA, "ka"), 32, 3, 2, RANK)
    (spread,) = call(collect_second_kernel, (got,), [(384, RANK)], "collect_b")
    got = exchange(spread, (*IA, "ka"), 32, 3, 4, RANK)

    loading_a, solved_b, chunk, gram_a = call(
        third_kernel,
        (coords, got, gram_c, solved_a, block),
        [(256, RANK), (256, RANK), (256, RANK), full],
        "third",
        1,
        [pltpu.VMEM((BI * BJ, RANK), BF16)],
    )
    got = exchange(chunk, (*IA, "ja"), 64, 4, RANK)
    (spread,) = call(collect_third_kernel, (got,), [(320, RANK)], "collect_c")
    same = exchange(spread, ("iy", "ja"), 32, 5, 2, RANK)
    other = lax.ppermute(same, "ic", [(0, 1), (1, 0)])

    loading_b, solved_c, squares = call(
        fourth_kernel,
        (same, other, gram_a, solved_b),
        [(256, RANK), (512, RANK), (1, RANK)],
        "fourth",
        0,
        [pltpu.VMEM((640, RANK), F32)],
    )
    total = squares
    for step in (1, 2, 3):
        total = total + lax.ppermute(squares, "ka", [(n, (n + step) % 4) for n in range(4)])
    loading_c = solved_c * lax.rsqrt(total / ROWS + EPSILON)
    return (loading_a, loading_b, loading_c)


def solution(mesh):
    shape = mesh.devices.shape
    split = jax.sharding.Mesh(
        mesh.devices.reshape(shape[0] // 2, 2, *shape[1:]), (*IA, "ja", "ka")
    )
    every = (*IA, "ja", "ka")
    placed = (P(every, None, None, None), P(None, every), P(every), P("ja", None), P("ka", None))
    return jax.shard_map(
        on_device,
        mesh=split,
        in_specs=placed,
        out_specs=(P(IA, None), P("ja", None), P("ka", None)),
        check_vma=False,
    )
```

```python
import jax
import jax.numpy as jnp
from jax import lax
from jax.experimental import pallas as pl
from jax.experimental.pallas import tpu as pltpu
from jax.sharding import PartitionSpec as P

RANK = 128
BI = 64
BJ = 64
BK = 128
GI_DEV = 4
GJ_DEV = 4
GK_DEV = 4
SLOTS = 4
ROWS = 2048
IA = ("iy", "ic")

RIDGE_SHARE = 0.3
EPSILON = 1e-06
HIGHEST = lax.Precision.HIGHEST
F32 = jnp.float32
BF16 = jnp.bfloat16


def exact_dot(left, right):
    return jnp.dot(left, right, precision=HIGHEST, preferred_element_type=F32)


def across_rows(left, right):
    return lax.dot_general(
        left, right, (((0,), (0,)), ((), ())), precision=HIGHEST, preferred_element_type=F32
    )


def gram(rows):
    return across_rows(rows, rows)


def halves(values):
    high = values.astype(BF16)
    return high, (values - high.astype(F32)).astype(BF16)


def iotas():
    shape = (RANK, RANK)
    return lax.broadcasted_iota(jnp.int32, shape, 0), lax.broadcasted_iota(jnp.int32, shape, 1)


def inverse(matrix):
    count = RANK // 8
    rows = [matrix[8 * n : 8 * n + 8, :] for n in range(count)]
    lane = lax.broadcasted_iota(jnp.int32, (8, RANK), 1)
    sub = lax.broadcasted_iota(jnp.int32, (8, RANK), 0)
    one = jnp.clip(rows[0], 1.0, 1.0)
    lefts, rights = [], []

    def over_lanes(tile, at):
        return jnp.broadcast_to(tile[:, at : at + 1], (8, RANK))

    def over_rows(tile, at):
        return jnp.broadcast_to(tile[at : at + 1, :], (8, RANK))

    for k in range(count // 2):
        low = 16 * k
        inside = (lane >= low) & (lane < low + 16)
        unit = [jnp.where(lane - low - 8 * h == sub, 1.0, 0.0) for h in range(2)]
        panel = rows[2 * k : 2 * k + 2]
        lefts += [jnp.where(lane < low, panel[h], unit[h]) for h in range(2)]
        columns = [[over_lanes(panel[h], low + t) * one for h in range(2)] for t in range(16)]
        panel = [jnp.where(inside, unit[h], panel[h]) for h in range(2)]
        for s in range(16):
            h, q = divmod(s, 8)
            pivot = over_rows(1.0 / columns[s][h], q)
            keep = jnp.where(sub == q, pivot, 1.0)
            here = jnp.where(sub == q, 0.0, columns[s][h]) * pivot
            there = columns[s][1 - h] * pivot

            def eliminate(pair):
                lead = over_rows(pair[h], q)
                result = [pair[h] * keep - here * lead, pair[1 - h] - there * lead]
                return result if h == 0 else result[::-1]

            panel = eliminate(panel)
            for t in range(s + 1, 16):
                columns[t] = eliminate(columns[t])
        rights += [jnp.where(lane < low + 16, panel[h], 0.0) for h in range(2)]
        rows[2 * k : 2 * k + 2] = panel
        leads = [over_rows(panel[s // 8], s % 8) for s in range(16)]
        for n in range(2 * k + 2, count):
            terms = [over_lanes(rows[n], low + s) * leads[s] for s in range(16)]
            while len(terms) > 1:
                terms = [terms[i] + terms[i + 1] for i in range(0, len(terms), 2)]
            rows[n] = jnp.where(inside, 0.0, rows[n]) - terms[0]
    return across_rows(jnp.concatenate(lefts, axis=0), jnp.concatenate(rights, axis=0))


def system_inverse(merged):
    row, col = iotas()
    shift = jnp.sum(jnp.where(row == col, merged, 0.0)) * (RIDGE_SHARE / RANK)
    return inverse(merged + jnp.where(row == col, shift, 0.0))


def strided(ref, start, count, step):
    return ref[pl.ds(start, count, stride=step), :]


def put(ref, start, count, step, value):
    ref[pl.ds(start, count, stride=step), :] = value


def scaled_gram(raw):
    row, col = iotas()
    diagonal = jnp.where(row == col, raw, 0.0)
    across = lax.rsqrt(jnp.sum(diagonal, axis=0, keepdims=True) + EPSILON)
    down = lax.rsqrt(jnp.sum(diagonal, axis=1, keepdims=True) + EPSILON)
    return across, raw * down * across


def places(coords_ref):
    at = [lax.axis_index(IA), lax.axis_index("ja"), lax.axis_index("ka")]
    return at, [coords_ref[n] - 4 * at[n] for n in range(3)]


def some_rows(ref, index, size):
    return ref[pl.ds(pl.multiple_of(index * size, size), size), :]


def first_kernel(
    coords_ref, block_ref, b_ref, c_ref, chunk_ref, y_ref,
    x_in, c_in, b_in, share_c, share_b, sems,
):
    at, slot = places(coords_ref)

    def window(ref, index, size):
        return ref.at[pl.ds(pl.multiple_of(index * size, size), size), :]

    small = [
        (window(c_ref, slot[2], BK), c_in),
        (window(b_ref, slot[1], BJ), b_in),
        (window(c_ref, at[1], 64), share_c),
        (window(b_ref, at[2], 64), share_b),
    ]
    parts = [pl.ds(n * (BI // 4), BI // 4) for n in range(4)]
    copies = [pltpu.make_async_copy(src, dst, sems.at[n]) for n, (src, dst) in enumerate(small)]
    copies += [
        pltpu.make_async_copy(block_ref.at[part], x_in.at[part], sems.at[4 + n])
        for n, part in enumerate(parts)
    ]
    for copy in copies:
        copy.start()
    for copy in copies[:4]:
        copy.wait()
    part_c = gram(share_c[...]) * (1.0 / ROWS)
    part_b = gram(share_b[...]) * (1.0 / ROWS)
    row, col = iotas()
    packed = jnp.where(row <= col, part_b, part_c)
    diagonal = jnp.sum(jnp.where(row == col, part_c, 0.0), axis=0, keepdims=True)
    for t in range(4):
        put(chunk_ref, 2 + t, 32, 8, packed[32 * t : 32 * t + 32])
    put(chunk_ref, 6, 32, 8, jnp.broadcast_to(diagonal, (32, RANK)))
    put(chunk_ref, 7, 32, 8, jnp.full((32, RANK), slot[0].astype(F32)))
    high, low = halves(c_in[...])
    both = jnp.concatenate([high, low], axis=0)
    rows_b = b_in[...]
    partial = []
    for n, part in enumerate(parts):
        copies[4 + n].wait()
        block = x_in[part].reshape(BI // 4 * BJ, BK)
        y = jnp.dot(jnp.concatenate([block, block], axis=1), both, preferred_element_type=F32)
        y = y.reshape(BI // 4, BJ, RANK)
        y_ref[part] = y
        partial += [jnp.sum(y[m] * rows_b, axis=0, keepdims=True) for m in range(BI // 4)]
    for t in range(2):
        put(chunk_ref, t, 32, 8, jnp.concatenate(partial[32 * t : 32 * t + 32], axis=0))


def collect(got_ref, count, step, ids, extras):
    rows = []
    for slot in range(SLOTS):
        for t in range(2):
            picked = jnp.where(ids == slot, strided(got_ref, t, count, step), 0.0)
            rows.append(jnp.sum(picked, axis=0, keepdims=True))
    for t in range(extras):
        rows.append(jnp.sum(strided(got_ref, 2 + t, count, step), axis=0, keepdims=True))
    return rows


def lower_lanes(values):
    lane = lax.broadcasted_iota(jnp.int32, values.shape, 1)
    return jnp.where(lane < 64, values, pltpu.roll(values, 64, 1))


def mark(rows, slot):
    lane = lax.broadcasted_iota(jnp.int32, rows.shape, 1)
    return jnp.where(lane < 64, slot.astype(F32), rows)


def unmark(raw):
    row, col = iotas()
    return jnp.where((row >= 64) & (col < 64), raw.T, raw)


def repeat_rows(ref, rows, copies):
    width = len(rows)
    unit = 1
    while width * unit % 8:
        unit *= 2
    tile = jnp.concatenate(rows * unit, axis=0)
    for n in range(copies // unit):
        ref[n * width * unit : (n + 1) * width * unit, :] = tile


def collect_first_kernel(got_ref, spread_ref, diagonal_ref):
    rows = collect(got_ref, 32, 8, strided(got_ref, 7, 32, 8), 5)
    repeat_rows(spread_ref, rows[:12], 32)
    diagonal_ref[...] = jnp.broadcast_to(rows[12], (8, RANK))


def collect_second_kernel(got_ref, spread_ref):
    rows = collect(got_ref, 32, 6, lower_lanes(strided(got_ref, 5, 32, 6)), 4)
    repeat_rows(spread_ref, rows, 32)


def collect_third_kernel(got_ref, spread_ref):
    rows = collect(got_ref, 64, 4, lower_lanes(strided(got_ref, 3, 64, 4)), 2)
    repeat_rows(spread_ref, rows, 32)


def natural(got_ref, count, step, first, last):
    return jnp.concatenate([strided(got_ref, t, count, step) for t in range(first, last)], axis=0)


def second_kernel(coords_ref, got_ref, diagonal_ref, y_ref, solved_ref, chunk_ref, gram_c_ref):
    at, slot = places(coords_ref)
    packed = natural(got_ref, 32, 12, 8, 12)
    flipped = packed.T
    row, col = iotas()
    gram_b = jnp.where(row <= col, packed, flipped)
    gram_c = jnp.where(row < col, flipped, packed)
    gram_c = jnp.where(row == col, diagonal_ref[0:1, :], gram_c)
    gram_c_ref[...] = gram_c
    solver = system_inverse(gram_b * gram_c)
    solved_ref[...] = exact_dot(natural(got_ref, 32, 12, 0, 8), solver)
    raw = gram(some_rows(solved_ref, at[2], 64)) * (1.0 / ROWS)
    own = some_rows(solved_ref, slot[0], BI)
    sums = [jnp.zeros((BJ, RANK), F32) for _ in range(2)]
    for n in range(BI):
        sums[n % 2] = sums[n % 2] + own[n : n + 1, :] * y_ref[n]
    partial = sums[0] + sums[1]
    for t in range(2):
        put(chunk_ref, t, 32, 6, partial[32 * t : 32 * t + 32])
    for t in range(4):
        rows = raw[32 * t : 32 * t + 32]
        put(chunk_ref, 2 + t, 32, 6, rows if t < 2 else mark(rows, slot[1]))


def third_kernel(
    coords_ref, got_ref, gram_c_ref, solved_a_ref, block_ref,
    loading_a_ref, solved_ref, chunk_ref, gram_a_ref, khatri_ref,
):
    at, slot = places(coords_ref)
    scale, gram_a = scaled_gram(unmark(natural(got_ref, 32, 12, 8, 12)))
    gram_a_ref[...] = gram_a
    loading_a_ref[...] = solved_a_ref[...] * scale
    solver = system_inverse(gram_a * gram_c_ref[...])
    solved_ref[...] = exact_dot(natural(got_ref, 32, 12, 0, 8) * scale, solver)
    raw = gram(some_rows(solved_ref, at[0], 32)) * (1.0 / ROWS)
    own_a = some_rows(loading_a_ref, slot[0], BI)
    own_b = some_rows(solved_ref, slot[1], BJ)
    for n in range(BI):
        khatri_ref[n * BJ : (n + 1) * BJ, :] = (own_a[n : n + 1, :] * own_b).astype(BF16)
    partial = lax.dot_general(
        block_ref[...].reshape(BI * BJ, BK),
        khatri_ref[...],
        (((0,), (0,)), ((), ())),
        preferred_element_type=F32,
    )
    for t in range(2):
        put(chunk_ref, t, 64, 4, partial[64 * t : 64 * t + 64])
    put(chunk_ref, 2, 64, 4, raw[0:64])
    put(chunk_ref, 3, 64, 4, mark(raw[64:128], slot[2]))


def fourth_kernel(
    same_ref, other_ref, gram_a_ref, solved_b_ref, loading_b_ref, solved_ref, squares_ref, rows_ref
):
    core = lax.axis_index("ic")
    for ref, half in ((same_ref, core), (other_ref, 1 - core)):
        for t in range(10):
            for n in range(4):
                place = pl.multiple_of(64 * t + 16 * n + 8 * half, 8)
                rows_ref[pl.ds(place, 8), :] = strided(ref, 80 * n + t, 8, 10)
    scale, gram_b = scaled_gram(unmark(rows_ref[512:640, :]))
    loading_b_ref[...] = solved_b_ref[...] * scale
    solver = system_inverse(gram_a_ref[...] * gram_b)
    solved = exact_dot(rows_ref[0:512, :] * scale, solver)
    solved_ref[...] = solved
    squares_ref[...] = jnp.sum(solved * solved, axis=0, keepdims=True)


def call(kernel, operands, outs, name, scalars=0, scratch=(), space=pltpu.VMEM):
    vmem = pl.BlockSpec(memory_space=pltpu.VMEM)
    smem = pl.BlockSpec(memory_space=pltpu.SMEM)
    return pl.pallas_call(
        kernel,
        out_shape=[jax.ShapeDtypeStruct(shape, F32) for shape in outs],
        in_specs=[smem] * scalars + [pl.BlockSpec(memory_space=space)] * (len(operands) - scalars),
        out_specs=[vmem] * len(outs),
        scratch_shapes=scratch,
        compiler_params=pltpu.CompilerParams(vmem_limit_bytes=32 << 20),
        name=name,
    )(*operands)


def exchange(values, axes, *chunk):
    shape = values.shape
    return lax.all_to_all(values.reshape(chunk), axes, 0, 0, tiled=True).reshape(shape)


def on_device(blocks, coords, live, factor_b, factor_c):
    block = blocks[0]
    coords = coords.reshape(3)
    full = (RANK, RANK)

    chunk, y = call(
        first_kernel,
        [pltpu.with_memory_space_constraint(v, pltpu.HBM) for v in (coords, block, factor_b, factor_c)],
        [(256, RANK), (BI, BJ, RANK)],
        "first",
        1,
        [
            pltpu.VMEM((BI, BJ, BK), BF16),
            pltpu.VMEM((BK, RANK), F32),
            pltpu.VMEM((BJ, RANK), F32),
            pltpu.VMEM((64, RANK), F32),
            pltpu.VMEM((64, RANK), F32),
            pltpu.SemaphoreType.DMA((8,)),
        ],
        pltpu.HBM,
    )
    got = exchange(chunk, ("ja", "ka"), 32, 8, RANK)
    spread, diagonal = call(collect_first_kernel, (got,), [(384, RANK), (8, RANK)], "collect_a")
    got = exchange(spread, ("ja", "ka"), 32, 3, 4, RANK)

    solved_a, chunk, gram_c = call(
        second_kernel, (coords, got, diagonal, y), [(256, RANK), (192, RANK), full], "second", 1
    )
    got = exchange(chunk, (*IA, "ka"), 32, 3, 2, RANK)
    (spread,) = call(collect_second_kernel, (got,), [(384, RANK)], "collect_b")
    got = exchange(spread, (*IA, "ka"), 32, 3, 4, RANK)

    loading_a, solved_b, chunk, gram_a = call(
        third_kernel,
        (coords, got, gram_c, solved_a, block),
        [(256, RANK), (256, RANK), (256, RANK), full],
        "third",
        1,
        [pltpu.VMEM((BI * BJ, RANK), BF16)],
    )
    got = exchange(chunk, (*IA, "ja"), 64, 4, RANK)
    (spread,) = call(collect_third_kernel, (got,), [(320, RANK)], "collect_c")
    same = exchange(spread, ("iy", "ja"), 32, 5, 2, RANK)
    other = lax.ppermute(same, "ic", [(0, 1), (1, 0)])

    loading_b, solved_c, squares = call(
        fourth_kernel,
        (same, other, gram_a, solved_b),
        [(256, RANK), (512, RANK), (1, RANK)],
        "fourth",
        0,
        [pltpu.VMEM((640, RANK), F32)],
    )
    total = squares
    for step in (1, 2, 3):
        total = total + lax.ppermute(squares, "ka", [(n, (n + step) % 4) for n in range(4)])
    loading_c = solved_c * lax.rsqrt(total / ROWS + EPSILON)
    return (loading_a, loading_b, loading_c)


def solution(mesh):
    shape = mesh.devices.shape
    split = jax.sharding.Mesh(
        mesh.devices.reshape(shape[0] // 2, 2, *shape[1:]), (*IA, "ja", "ka")
    )
    every = (*IA, "ja", "ka")
    placed = (P(every, None, None, None), P(None, every), P(every), P("ja", None), P("ka", None))
    return jax.shard_map(
        on_device,
        mesh=split,
        in_specs=placed,
        out_specs=(P(IA, None), P("ja", None), P("ka", None)),
        check_vma=False,
    )
```

```python
import jax
import jax.numpy as jnp
from jax import lax
from jax.experimental import pallas as pl
from jax.experimental.pallas import tpu as pltpu
from jax.sharding import PartitionSpec as P

RANK = 128
BI = 64
BJ = 64
BK = 128
GI_DEV = 4
GJ_DEV = 4
GK_DEV = 4
SLOTS = 4
ROWS = 2048
IA = ("iy", "ic")

RIDGE_SHARE = 0.3
EPSILON = 1e-06
HIGHEST = lax.Precision.HIGHEST
F32 = jnp.float32
BF16 = jnp.bfloat16


def exact_dot(left, right):
    return jnp.dot(left, right, precision=HIGHEST, preferred_element_type=F32)


def across_rows(left, right):
    return lax.dot_general(
        left, right, (((0,), (0,)), ((), ())), precision=HIGHEST, preferred_element_type=F32
    )


def gram(rows):
    return across_rows(rows, rows)


def halves(values):
    high = values.astype(BF16)
    return high, (values - high.astype(F32)).astype(BF16)


def iotas():
    shape = (RANK, RANK)
    return lax.broadcasted_iota(jnp.int32, shape, 0), lax.broadcasted_iota(jnp.int32, shape, 1)


def inverse(matrix):
    count = RANK // 8
    rows = [matrix[8 * n : 8 * n + 8, :] for n in range(count)]
    lane = lax.broadcasted_iota(jnp.int32, (8, RANK), 1)
    sub = lax.broadcasted_iota(jnp.int32, (8, RANK), 0)
    one = jnp.clip(rows[0], 1.0, 1.0)
    lefts, rights = [], []

    def over_lanes(tile, at):
        return jnp.broadcast_to(tile[:, at : at + 1], (8, RANK))

    def over_rows(tile, at):
        return jnp.broadcast_to(tile[at : at + 1, :], (8, RANK))

    for k in range(count // 2):
        low = 16 * k
        inside = (lane >= low) & (lane < low + 16)
        unit = [jnp.where(lane - low - 8 * h == sub, 1.0, 0.0) for h in range(2)]
        panel = rows[2 * k : 2 * k + 2]
        lefts += [jnp.where(lane < low, panel[h], unit[h]) for h in range(2)]
        columns = [[over_lanes(panel[h], low + t) * one for h in range(2)] for t in range(16)]
        panel = [jnp.where(inside, unit[h], panel[h]) for h in range(2)]
        for s in range(16):
            h, q = divmod(s, 8)
            pivot = over_rows(1.0 / columns[s][h], q)
            keep = jnp.where(sub == q, pivot, 1.0)
            here = jnp.where(sub == q, 0.0, columns[s][h]) * pivot
            there = columns[s][1 - h] * pivot

            def eliminate(pair):
                lead = over_rows(pair[h], q)
                result = [pair[h] * keep - here * lead, pair[1 - h] - there * lead]
                return result if h == 0 else result[::-1]

            panel = eliminate(panel)
            for t in range(s + 1, 16):
                columns[t] = eliminate(columns[t])
        rights += [jnp.where(lane < low + 16, panel[h], 0.0) for h in range(2)]
        rows[2 * k : 2 * k + 2] = panel
        leads = [over_rows(panel[s // 8], s % 8) for s in range(16)]
        for n in range(2 * k + 2, count):
            terms = [over_lanes(rows[n], low + s) * leads[s] for s in range(16)]
            while len(terms) > 1:
                terms = [terms[i] + terms[i + 1] for i in range(0, len(terms), 2)]
            rows[n] = jnp.where(inside, 0.0, rows[n]) - terms[0]
    return across_rows(jnp.concatenate(lefts, axis=0), jnp.concatenate(rights, axis=0))


def system_inverse(merged):
    row, col = iotas()
    shift = jnp.sum(jnp.where(row == col, merged, 0.0)) * (RIDGE_SHARE / RANK)
    return inverse(merged + jnp.where(row == col, shift, 0.0))


def strided(ref, start, count, step):
    return ref[pl.ds(start, count, stride=step), :]


def put(ref, start, count, step, value):
    ref[pl.ds(start, count, stride=step), :] = value


def scaled_gram(raw):
    row, col = iotas()
    diagonal = jnp.where(row == col, raw, 0.0)
    across = lax.rsqrt(jnp.sum(diagonal, axis=0, keepdims=True) + EPSILON)
    down = lax.rsqrt(jnp.sum(diagonal, axis=1, keepdims=True) + EPSILON)
    return across, raw * down * across


def places(coords_ref):
    at = [lax.axis_index(IA), lax.axis_index("ja"), lax.axis_index("ka")]
    return at, [coords_ref[n] - 4 * at[n] for n in range(3)]


def some_rows(ref, index, size):
    return ref[pl.ds(pl.multiple_of(index * size, size), size), :]


def first_kernel(
    coords_ref, block_ref, b_ref, c_ref, chunk_ref, y_ref,
    x_in, c_in, b_in, share_c, share_b, sems,
):
    at, slot = places(coords_ref)

    def window(ref, index, size):
        return ref.at[pl.ds(pl.multiple_of(index * size, size), size), :]

    small = [
        (window(c_ref, slot[2], BK), c_in),
        (window(b_ref, slot[1], BJ), b_in),
        (window(c_ref, at[1], 64), share_c),
        (window(b_ref, at[2], 64), share_b),
    ]
    parts = [pl.ds(n * (BI // 4), BI // 4) for n in range(4)]
    copies = [pltpu.make_async_copy(src, dst, sems.at[n]) for n, (src, dst) in enumerate(small)]
    copies += [
        pltpu.make_async_copy(block_ref.at[part], x_in.at[part], sems.at[4 + n])
        for n, part in enumerate(parts)
    ]
    for copy in copies:
        copy.start()
    for copy in copies[:4]:
        copy.wait()
    part_c = gram(share_c[...]) * (1.0 / ROWS)
    part_b = gram(share_b[...]) * (1.0 / ROWS)
    row, col = iotas()
    packed = jnp.where(row <= col, part_b, part_c)
    diagonal = jnp.sum(jnp.where(row == col, part_c, 0.0), axis=0, keepdims=True)
    for t in range(4):
        put(chunk_ref, 2 + t, 32, 8, packed[32 * t : 32 * t + 32])
    put(chunk_ref, 6, 32, 8, jnp.broadcast_to(diagonal, (32, RANK)))
    put(chunk_ref, 7, 32, 8, jnp.full((32, RANK), slot[0].astype(F32)))
    high, low = halves(c_in[...])
    both = jnp.concatenate([high, low], axis=0)
    rows_b = b_in[...]
    partial = []
    for n, part in enumerate(parts):
        copies[4 + n].wait()
        block = x_in[part].reshape(BI // 4 * BJ, BK)
        y = jnp.dot(jnp.concatenate([block, block], axis=1), both, preferred_element_type=F32)
        y = y.reshape(BI // 4, BJ, RANK)
        y_ref[part] = y
        partial += [jnp.sum(y[m] * rows_b, axis=0, keepdims=True) for m in range(BI // 4)]
    for t in range(2):
        put(chunk_ref, t, 32, 8, jnp.concatenate(partial[32 * t : 32 * t + 32], axis=0))


def collect(got_ref, count, step, ids, extras):
    rows = []
    for slot in range(SLOTS):
        for t in range(2):
            picked = jnp.where(ids == slot, strided(got_ref, t, count, step), 0.0)
            rows.append(jnp.sum(picked, axis=0, keepdims=True))
    for t in range(extras):
        rows.append(jnp.sum(strided(got_ref, 2 + t, count, step), axis=0, keepdims=True))
    return rows


def lower_lanes(values):
    lane = lax.broadcasted_iota(jnp.int32, values.shape, 1)
    return jnp.where(lane < 64, values, pltpu.roll(values, 64, 1))


def mark(rows, slot):
    lane = lax.broadcasted_iota(jnp.int32, rows.shape, 1)
    return jnp.where(lane < 64, slot.astype(F32), rows)


def unmark(raw):
    row, col = iotas()
    return jnp.where((row >= 64) & (col < 64), raw.T, raw)


def repeat_rows(ref, rows, copies):
    width = len(rows)
    unit = 1
    while width * unit % 8:
        unit *= 2
    tile = jnp.concatenate(rows * unit, axis=0)
    for n in range(copies // unit):
        ref[n * width * unit : (n + 1) * width * unit, :] = tile


def collect_first_kernel(got_ref, spread_ref, diagonal_ref):
    rows = collect(got_ref, 32, 8, strided(got_ref, 7, 32, 8), 5)
    repeat_rows(spread_ref, rows[:12], 32)
    diagonal_ref[...] = jnp.broadcast_to(rows[12], (8, RANK))


def collect_second_kernel(got_ref, half_ref):
    sums = [jnp.zeros((32, RANK), F32) for _ in range(SLOTS)]
    for n in range(16):
        for part in range(2):
            start = 88 * n + 32 * part
            rows = got_ref[start : start + 32, :]
            ids = got_ref[88 * n + 80 + part : 88 * n + 81 + part, :]
            for slot in range(SLOTS):
                sums[slot] = sums[slot] + jnp.where(ids == slot, rows, 0.0)
    for slot in range(SLOTS):
        half_ref[32 * slot : 32 * slot + 32, :] = sums[slot]
    for share in range(4):
        starts = [88 * (4 * n + share) + 64 for n in range(4)]
        total = [got_ref[start : start + 16, :] for start in starts]
        half_ref[128 + 16 * share : 144 + 16 * share, :] = (total[0] + total[1]) + (total[2] + total[3])


def collect_third_kernel(got_ref, spread_ref):
    rows = collect(got_ref, 64, 4, lower_lanes(strided(got_ref, 3, 64, 4)), 2)
    repeat_rows(spread_ref, rows, 32)


def natural(got_ref, count, step, first, last):
    return jnp.concatenate([strided(got_ref, t, count, step) for t in range(first, last)], axis=0)


def second_kernel(
    coords_ref, got_ref, diagonal_ref, y_ref,
    solved_ref, gram_c_ref, keep_ref, send_ref, partial_ref, raw_ref,
):
    at, slot = places(coords_ref)
    packed = natural(got_ref, 32, 12, 8, 12)
    flipped = packed.T
    row, col = iotas()
    gram_b = jnp.where(row <= col, packed, flipped)
    gram_c = jnp.where(row < col, flipped, packed)
    gram_c = jnp.where(row == col, diagonal_ref[0:1, :], gram_c)
    gram_c_ref[...] = gram_c
    solver = system_inverse(gram_b * gram_c)
    solved = exact_dot(natural(got_ref, 32, 12, 0, 8), solver)
    solved_ref[...] = solved
    raw_ref[...] = gram(solved) * (1.0 / ROWS)
    own = some_rows(solved_ref, slot[0], BI)
    sums = [jnp.zeros((BJ, RANK), F32) for _ in range(2)]
    for n in range(BI):
        sums[n % 2] = sums[n % 2] + own[n : n + 1, :] * y_ref[n]
    partial_ref[...] = sums[0] + sums[1]
    core = lax.axis_index("ic")
    for ref, half in ((keep_ref, core), (send_ref, 1 - core)):
        ref[0:32, :] = some_rows(partial_ref, half, 32)
        ref[32:48, :] = some_rows(raw_ref, 4 * half + at[2], 16)
        ref[48:56, :] = jnp.full((8, RANK), slot[1].astype(F32))


def merge_kernel(keep_ref, other_ref, spread_ref):
    first = lax.broadcasted_iota(jnp.int32, (8, RANK), 0) == 0
    tile = [
        keep_ref[0:32, :],
        other_ref[0:32, :],
        keep_ref[32:48, :] + other_ref[32:48, :],
        jnp.where(first, keep_ref[48:56, :], other_ref[48:56, :]),
    ]
    tile = jnp.concatenate(tile, axis=0)
    for n in range(16):
        spread_ref[88 * n : 88 * n + 88, :] = tile


def third_kernel(
    coords_ref, same_ref, other_ref, gram_c_ref, solved_a_ref, block_ref,
    loading_a_ref, solved_ref, chunk_ref, gram_a_ref, khatri_ref, rows_ref,
):
    at, slot = places(coords_ref)
    core = lax.axis_index("ic")
    for ref, half in ((same_ref, core), (other_ref, 1 - core)):
        for n in range(SLOTS):
            place = pl.multiple_of(64 * n + 32 * half, 32)
            rows_ref[pl.ds(place, 32), :] = ref[32 * n : 32 * n + 32, :]
        rows_ref[pl.ds(pl.multiple_of(256 + 64 * half, 64), 64), :] = ref[128:192, :]
    scale, gram_a = scaled_gram(rows_ref[256:384, :])
    gram_a_ref[...] = gram_a
    loading_a_ref[...] = solved_a_ref[...] * scale
    solver = system_inverse(gram_a * gram_c_ref[...])
    solved_ref[...] = exact_dot(rows_ref[0:256, :] * scale, solver)
    raw = gram(some_rows(solved_ref, at[0], 32)) * (1.0 / ROWS)
    own_a = some_rows(loading_a_ref, slot[0], BI)
    own_b = some_rows(solved_ref, slot[1], BJ)
    for n in range(BI):
        khatri_ref[n * BJ : (n + 1) * BJ, :] = (own_a[n : n + 1, :] * own_b).astype(BF16)
    partial = lax.dot_general(
        block_ref[...].reshape(BI * BJ, BK),
        khatri_ref[...],
        (((0,), (0,)), ((), ())),
        preferred_element_type=F32,
    )
    for t in range(2):
        put(chunk_ref, t, 64, 4, partial[64 * t : 64 * t + 64])
    put(chunk_ref, 2, 64, 4, raw[0:64])
    put(chunk_ref, 3, 64, 4, mark(raw[64:128], slot[2]))


def fourth_kernel(
    same_ref, other_ref, gram_a_ref, solved_b_ref, loading_b_ref, solved_ref, squares_ref, rows_ref
):
    core = lax.axis_index("ic")
    for ref, half in ((same_ref, core), (other_ref, 1 - core)):
        for t in range(10):
            for n in range(4):
                place = pl.multiple_of(64 * t + 16 * n + 8 * half, 8)
                rows_ref[pl.ds(place, 8), :] = strided(ref, 80 * n + t, 8, 10)
    scale, gram_b = scaled_gram(unmark(rows_ref[512:640, :]))
    loading_b_ref[...] = solved_b_ref[...] * scale
    solver = system_inverse(gram_a_ref[...] * gram_b)
    solved = exact_dot(rows_ref[0:512, :] * scale, solver)
    solved_ref[...] = solved
    squares_ref[...] = jnp.sum(solved * solved, axis=0, keepdims=True)


def call(kernel, operands, outs, name, scalars=0, scratch=(), space=pltpu.VMEM):
    vmem = pl.BlockSpec(memory_space=pltpu.VMEM)
    smem = pl.BlockSpec(memory_space=pltpu.SMEM)
    return pl.pallas_call(
        kernel,
        out_shape=[jax.ShapeDtypeStruct(shape, F32) for shape in outs],
        in_specs=[smem] * scalars + [pl.BlockSpec(memory_space=space)] * (len(operands) - scalars),
        out_specs=[vmem] * len(outs),
        scratch_shapes=scratch,
        compiler_params=pltpu.CompilerParams(vmem_limit_bytes=32 << 20),
        name=name,
    )(*operands)


def exchange(values, axes, *chunk):
    shape = values.shape
    return lax.all_to_all(values.reshape(chunk), axes, 0, 0, tiled=True).reshape(shape)


def swap_cores(values):
    return lax.ppermute(values, "ic", [(0, 1), (1, 0)])


def on_device(blocks, coords, live, factor_b, factor_c):
    block = blocks[0]
    coords = coords.reshape(3)
    full = (RANK, RANK)

    chunk, y = call(
        first_kernel,
        [pltpu.with_memory_space_constraint(v, pltpu.HBM) for v in (coords, block, factor_b, factor_c)],
        [(256, RANK), (BI, BJ, RANK)],
        "first",
        1,
        [
            pltpu.VMEM((BI, BJ, BK), BF16),
            pltpu.VMEM((BK, RANK), F32),
            pltpu.VMEM((BJ, RANK), F32),
            pltpu.VMEM((64, RANK), F32),
            pltpu.VMEM((64, RANK), F32),
            pltpu.SemaphoreType.DMA((8,)),
        ],
        pltpu.HBM,
    )
    got = exchange(chunk, ("ja", "ka"), 32, 8, RANK)
    spread, diagonal = call(collect_first_kernel, (got,), [(384, RANK), (8, RANK)], "collect_a")
    got = exchange(spread, ("ja", "ka"), 32, 3, 4, RANK)

    solved_a, gram_c, keep, send = call(
        second_kernel,
        (coords, got, diagonal, y),
        [(256, RANK), full, (56, RANK), (56, RANK)],
        "second",
        1,
        [pltpu.VMEM((BJ, RANK), F32), pltpu.VMEM(full, F32)],
    )
    (spread,) = call(merge_kernel, (keep, swap_cores(send)), [(1408, RANK)], "merge")
    got = exchange(spread, ("iy", "ka"), 16, 88, RANK)
    (half,) = call(collect_second_kernel, (got,), [(192, RANK)], "collect_b")

    loading_a, solved_b, chunk, gram_a = call(
        third_kernel,
        (coords, half, swap_cores(half), gram_c, solved_a, block),
        [(256, RANK), (256, RANK), (256, RANK), full],
        "third",
        1,
        [pltpu.VMEM((BI * BJ, RANK), BF16), pltpu.VMEM((384, RANK), F32)],
    )
    got = exchange(chunk, (*IA, "ja"), 64, 4, RANK)
    (spread,) = call(collect_third_kernel, (got,), [(320, RANK)], "collect_c")
    same = exchange(spread, ("iy", "ja"), 32, 5, 2, RANK)
    other = swap_cores(same)

    loading_b, solved_c, squares = call(
        fourth_kernel,
        (same, other, gram_a, solved_b),
        [(256, RANK), (512, RANK), (1, RANK)],
        "fourth",
        0,
        [pltpu.VMEM((640, RANK), F32)],
    )
    total = squares
    for step in (1, 2, 3):
        total = total + lax.ppermute(squares, "ka", [(n, (n + step) % 4) for n in range(4)])
    loading_c = solved_c * lax.rsqrt(total / ROWS + EPSILON)
    return (loading_a, loading_b, loading_c)


def solution(mesh):
    shape = mesh.devices.shape
    split = jax.sharding.Mesh(
        mesh.devices.reshape(shape[0] // 2, 2, *shape[1:]), (*IA, "ja", "ka")
    )
    every = (*IA, "ja", "ka")
    placed = (P(every, None, None, None), P(None, every), P(every), P("ja", None), P("ka", None))
    return jax.shard_map(
        on_device,
        mesh=split,
        in_specs=placed,
        out_specs=(P(IA, None), P("ja", None), P("ka", None)),
        check_vma=False,
    )
```

```python
import jax
import jax.numpy as jnp
from jax import lax
from jax.experimental import pallas as pl
from jax.experimental.pallas import tpu as pltpu
from jax.sharding import PartitionSpec as P

RANK = 128
BI = 64
BJ = 64
BK = 128
GI_DEV = 4
GJ_DEV = 4
GK_DEV = 4
SLOTS = 4
ROWS = 2048
IA = ("iy", "ic")

RIDGE_SHARE = 0.3
EPSILON = 1e-06
HIGHEST = lax.Precision.HIGHEST
F32 = jnp.float32
BF16 = jnp.bfloat16


def exact_dot(left, right):
    return jnp.dot(left, right, precision=HIGHEST, preferred_element_type=F32)


def across_rows(left, right):
    return lax.dot_general(
        left, right, (((0,), (0,)), ((), ())), precision=HIGHEST, preferred_element_type=F32
    )


def gram(rows):
    return across_rows(rows, rows)


def halves(values):
    high = values.astype(BF16)
    return high, (values - high.astype(F32)).astype(BF16)


def iotas():
    shape = (RANK, RANK)
    return lax.broadcasted_iota(jnp.int32, shape, 0), lax.broadcasted_iota(jnp.int32, shape, 1)


def inverse(matrix):
    count = RANK // 8
    rows = [matrix[8 * n : 8 * n + 8, :] for n in range(count)]
    lane = lax.broadcasted_iota(jnp.int32, (8, RANK), 1)
    sub = lax.broadcasted_iota(jnp.int32, (8, RANK), 0)
    one = jnp.clip(rows[0], 1.0, 1.0)
    lefts, rights = [], []

    def over_lanes(tile, at):
        return jnp.broadcast_to(tile[:, at : at + 1], (8, RANK))

    def over_rows(tile, at):
        return jnp.broadcast_to(tile[at : at + 1, :], (8, RANK))

    for k in range(count // 2):
        low = 16 * k
        inside = (lane >= low) & (lane < low + 16)
        unit = [jnp.where(lane - low - 8 * h == sub, 1.0, 0.0) for h in range(2)]
        panel = rows[2 * k : 2 * k + 2]
        lefts += [jnp.where(lane < low, panel[h], unit[h]) for h in range(2)]
        columns = [[over_lanes(panel[h], low + t) * one for h in range(2)] for t in range(16)]
        panel = [jnp.where(inside, unit[h], panel[h]) for h in range(2)]
        for s in range(16):
            h, q = divmod(s, 8)
            pivot = over_rows(1.0 / columns[s][h], q)
            keep = jnp.where(sub == q, pivot, 1.0)
            here = jnp.where(sub == q, 0.0, columns[s][h]) * pivot
            there = columns[s][1 - h] * pivot

            def eliminate(pair):
                lead = over_rows(pair[h], q)
                result = [pair[h] * keep - here * lead, pair[1 - h] - there * lead]
                return result if h == 0 else result[::-1]

            panel = eliminate(panel)
            for t in range(s + 1, 16):
                columns[t] = eliminate(columns[t])
        rights += [jnp.where(lane < low + 16, panel[h], 0.0) for h in range(2)]
        rows[2 * k : 2 * k + 2] = panel
        leads = [over_rows(panel[s // 8], s % 8) for s in range(16)]
        for n in range(2 * k + 2, count):
            terms = [over_lanes(rows[n], low + s) * leads[s] for s in range(16)]
            while len(terms) > 1:
                terms = [terms[i] + terms[i + 1] for i in range(0, len(terms), 2)]
            rows[n] = jnp.where(inside, 0.0, rows[n]) - terms[0]
    return across_rows(jnp.concatenate(lefts, axis=0), jnp.concatenate(rights, axis=0))


def system_inverse(merged):
    row, col = iotas()
    shift = jnp.sum(jnp.where(row == col, merged, 0.0)) * (RIDGE_SHARE / RANK)
    return inverse(merged + jnp.where(row == col, shift, 0.0))


def strided(ref, start, count, step):
    return ref[pl.ds(start, count, stride=step), :]


def put(ref, start, count, step, value):
    ref[pl.ds(start, count, stride=step), :] = value


def scaled_gram(raw):
    row, col = iotas()
    diagonal = jnp.where(row == col, raw, 0.0)
    across = lax.rsqrt(jnp.sum(diagonal, axis=0, keepdims=True) + EPSILON)
    down = lax.rsqrt(jnp.sum(diagonal, axis=1, keepdims=True) + EPSILON)
    return across, raw * down * across


def places(coords_ref):
    at = [lax.axis_index(IA), lax.axis_index("ja"), lax.axis_index("ka")]
    return at, [coords_ref[n] - 4 * at[n] for n in range(3)]


def some_rows(ref, index, size):
    return ref[pl.ds(pl.multiple_of(index * size, size), size), :]


def first_kernel(
    coords_ref, block_ref, b_ref, c_ref, chunk_ref, y_ref,
    x_in, c_in, b_in, share_c, share_b, sems,
):
    at, slot = places(coords_ref)

    def window(ref, index, size):
        return ref.at[pl.ds(pl.multiple_of(index * size, size), size), :]

    small = [
        (window(c_ref, slot[2], BK), c_in),
        (window(b_ref, slot[1], BJ), b_in),
        (window(c_ref, at[1], 64), share_c),
        (window(b_ref, at[2], 64), share_b),
    ]
    parts = [pl.ds(n * (BI // 4), BI // 4) for n in range(4)]
    copies = [pltpu.make_async_copy(src, dst, sems.at[n]) for n, (src, dst) in enumerate(small)]
    copies += [
        pltpu.make_async_copy(block_ref.at[part], x_in.at[part], sems.at[4 + n])
        for n, part in enumerate(parts)
    ]
    for copy in copies:
        copy.start()
    for copy in copies[:4]:
        copy.wait()
    part_c = gram(share_c[...]) * (1.0 / ROWS)
    part_b = gram(share_b[...]) * (1.0 / ROWS)
    row, col = iotas()
    packed = jnp.where(row <= col, part_b, part_c)
    diagonal = jnp.sum(jnp.where(row == col, part_c, 0.0), axis=0, keepdims=True)
    for t in range(4):
        put(chunk_ref, 2 + t, 32, 8, packed[32 * t : 32 * t + 32])
    put(chunk_ref, 6, 32, 8, jnp.broadcast_to(diagonal, (32, RANK)))
    put(chunk_ref, 7, 32, 8, jnp.full((32, RANK), slot[0].astype(F32)))
    high, low = halves(c_in[...])
    both = jnp.concatenate([high, low], axis=0)
    rows_b = b_in[...]
    partial = []
    for n, part in enumerate(parts):
        copies[4 + n].wait()
        block = x_in[part].reshape(BI // 4 * BJ, BK)
        y = jnp.dot(jnp.concatenate([block, block], axis=1), both, preferred_element_type=F32)
        y = y.reshape(BI // 4, BJ, RANK)
        y_ref[part] = y
        partial += [jnp.sum(y[m] * rows_b, axis=0, keepdims=True) for m in range(BI // 4)]
    for t in range(2):
        put(chunk_ref, t, 32, 8, jnp.concatenate(partial[32 * t : 32 * t + 32], axis=0))


def collect(got_ref, count, step, ids, extras):
    rows = []
    for slot in range(SLOTS):
        for t in range(2):
            picked = jnp.where(ids == slot, strided(got_ref, t, count, step), 0.0)
            rows.append(jnp.sum(picked, axis=0, keepdims=True))
    for t in range(extras):
        rows.append(jnp.sum(strided(got_ref, 2 + t, count, step), axis=0, keepdims=True))
    return rows


def lower_lanes(values):
    lane = lax.broadcasted_iota(jnp.int32, values.shape, 1)
    return jnp.where(lane < 64, values, pltpu.roll(values, 64, 1))


def mark(rows, slot):
    lane = lax.broadcasted_iota(jnp.int32, rows.shape, 1)
    return jnp.where(lane < 64, slot.astype(F32), rows)


def unmark(raw):
    row, col = iotas()
    return jnp.where((row >= 64) & (col < 64), raw.T, raw)


def repeat_rows(ref, rows, copies):
    width = len(rows)
    unit = 1
    while width * unit % 8:
        unit *= 2
    tile = jnp.concatenate(rows * unit, axis=0)
    for n in range(copies // unit):
        ref[n * width * unit : (n + 1) * width * unit, :] = tile


def collect_first_kernel(got_ref, spread_ref, diagonal_ref):
    rows = collect(got_ref, 32, 8, strided(got_ref, 7, 32, 8), 5)
    repeat_rows(spread_ref, rows[:12], 32)
    diagonal_ref[...] = jnp.broadcast_to(rows[12], (8, RANK))


def collect_third_kernel(got_ref, spread_ref):
    rows = collect(got_ref, 64, 4, lower_lanes(strided(got_ref, 3, 64, 4)), 2)
    repeat_rows(spread_ref, rows, 32)


def natural(got_ref, count, step, first, last):
    return jnp.concatenate([strided(got_ref, t, count, step) for t in range(first, last)], axis=0)


def second_kernel(
    coords_ref, got_ref, diagonal_ref, y_ref,
    solved_ref, gram_c_ref, keep_ref, send_ref, partial_ref, raw_ref,
):
    at, slot = places(coords_ref)
    packed = natural(got_ref, 32, 12, 8, 12)
    flipped = packed.T
    row, col = iotas()
    gram_b = jnp.where(row <= col, packed, flipped)
    gram_c = jnp.where(row < col, flipped, packed)
    gram_c = jnp.where(row == col, diagonal_ref[0:1, :], gram_c)
    gram_c_ref[...] = gram_c
    solver = system_inverse(gram_b * gram_c)
    solved = exact_dot(natural(got_ref, 32, 12, 0, 8), solver)
    solved_ref[...] = solved
    raw_ref[...] = gram(solved) * (1.0 / ROWS)
    own = some_rows(solved_ref, slot[0], BI)
    sums = [jnp.zeros((BJ, RANK), F32) for _ in range(2)]
    for n in range(BI):
        sums[n % 2] = sums[n % 2] + own[n : n + 1, :] * y_ref[n]
    partial_ref[...] = sums[0] + sums[1]
    core = lax.axis_index("ic")
    for ref, half in ((keep_ref, core), (send_ref, 1 - core)):
        ref[0:32, :] = some_rows(partial_ref, half, 32)
        ref[32:96, :] = some_rows(raw_ref, half, 64)
        ref[96:104, :] = jnp.full((8, RANK), slot[1].astype(F32))


def merge_kernel(keep_ref, other_ref, parts_ref, gram_ref):
    first = lax.broadcasted_iota(jnp.int32, (8, RANK), 0) == 0
    parts_ref[0:32, :] = keep_ref[0:32, :]
    parts_ref[32:64, :] = other_ref[0:32, :]
    parts_ref[64:72, :] = jnp.where(first, keep_ref[96:104, :], other_ref[96:104, :])
    gram_ref[...] = keep_ref[32:96, :] + other_ref[32:96, :]


def in_source_order(axis, refs, all_ref):
    size = refs[0].shape[0]
    me = lax.axis_index(axis)
    for step, ref in enumerate(refs):
        source = lax.rem(me + 4 - step, 4)
        all_ref[pl.ds(pl.multiple_of(source * size, 8), size), :] = ref[...]


def dense_kernel(parts_0, parts_1, parts_2, parts_3, gram_ref, half_ref, all_ref):
    in_source_order("ka", (parts_0, parts_1, parts_2, parts_3), all_ref)
    sums = [jnp.zeros((32, RANK), F32) for _ in range(SLOTS)]
    for n in range(4):
        for part in range(2):
            rows = all_ref[72 * n + 32 * part : 72 * n + 32 * part + 32, :]
            ids = all_ref[72 * n + 64 + part : 72 * n + 65 + part, :]
            for slot in range(SLOTS):
                sums[slot] = sums[slot] + jnp.where(ids == slot, rows, 0.0)
    for slot in range(SLOTS):
        half_ref[32 * slot : 32 * slot + 32, :] = sums[slot]
    half_ref[128:192, :] = gram_ref[...]


def sum_kernel(half_0, half_1, half_2, half_3, sum_ref, all_ref):
    in_source_order("iy", (half_0, half_1, half_2, half_3), all_ref)
    parts = [all_ref[192 * n : 192 * n + 192, :] for n in range(4)]
    sum_ref[...] = (parts[0] + parts[1]) + (parts[2] + parts[3])


def third_kernel(
    coords_ref, same_ref, other_ref, gram_c_ref, solved_a_ref, block_ref,
    loading_a_ref, solved_ref, chunk_ref, gram_a_ref, khatri_ref, rows_ref,
):
    at, slot = places(coords_ref)
    core = lax.axis_index("ic")
    for ref, half in ((same_ref, core), (other_ref, 1 - core)):
        for n in range(SLOTS):
            place = pl.multiple_of(64 * n + 32 * half, 32)
            rows_ref[pl.ds(place, 32), :] = ref[32 * n : 32 * n + 32, :]
        rows_ref[pl.ds(pl.multiple_of(256 + 64 * half, 64), 64), :] = ref[128:192, :]
    scale, gram_a = scaled_gram(rows_ref[256:384, :])
    gram_a_ref[...] = gram_a
    loading_a_ref[...] = solved_a_ref[...] * scale
    solver = system_inverse(gram_a * gram_c_ref[...])
    solved_ref[...] = exact_dot(rows_ref[0:256, :] * scale, solver)
    raw = gram(some_rows(solved_ref, at[0], 32)) * (1.0 / ROWS)
    own_a = some_rows(loading_a_ref, slot[0], BI)
    own_b = some_rows(solved_ref, slot[1], BJ)
    for n in range(BI):
        khatri_ref[n * BJ : (n + 1) * BJ, :] = (own_a[n : n + 1, :] * own_b).astype(BF16)
    partial = lax.dot_general(
        block_ref[...].reshape(BI * BJ, BK),
        khatri_ref[...],
        (((0,), (0,)), ((), ())),
        preferred_element_type=F32,
    )
    for t in range(2):
        put(chunk_ref, t, 64, 4, partial[64 * t : 64 * t + 64])
    put(chunk_ref, 2, 64, 4, raw[0:64])
    put(chunk_ref, 3, 64, 4, mark(raw[64:128], slot[2]))


def fourth_kernel(
    same_ref, other_ref, gram_a_ref, solved_b_ref, loading_b_ref, solved_ref, squares_ref, rows_ref
):
    core = lax.axis_index("ic")
    for ref, half in ((same_ref, core), (other_ref, 1 - core)):
        for t in range(10):
            for n in range(4):
                place = pl.multiple_of(64 * t + 16 * n + 8 * half, 8)
                rows_ref[pl.ds(place, 8), :] = strided(ref, 80 * n + t, 8, 10)
    scale, gram_b = scaled_gram(unmark(rows_ref[512:640, :]))
    loading_b_ref[...] = solved_b_ref[...] * scale
    solver = system_inverse(gram_a_ref[...] * gram_b)
    solved = exact_dot(rows_ref[0:512, :] * scale, solver)
    solved_ref[...] = solved
    squares_ref[...] = jnp.sum(solved * solved, axis=0, keepdims=True)


def call(kernel, operands, outs, name, scalars=0, scratch=(), space=pltpu.VMEM):
    vmem = pl.BlockSpec(memory_space=pltpu.VMEM)
    smem = pl.BlockSpec(memory_space=pltpu.SMEM)
    return pl.pallas_call(
        kernel,
        out_shape=[jax.ShapeDtypeStruct(shape, F32) for shape in outs],
        in_specs=[smem] * scalars + [pl.BlockSpec(memory_space=space)] * (len(operands) - scalars),
        out_specs=[vmem] * len(outs),
        scratch_shapes=scratch,
        compiler_params=pltpu.CompilerParams(vmem_limit_bytes=32 << 20),
        name=name,
    )(*operands)


def exchange(values, axes, *chunk):
    shape = values.shape
    return lax.all_to_all(values.reshape(chunk), axes, 0, 0, tiled=True).reshape(shape)


def swap_cores(values):
    return lax.ppermute(values, "ic", [(0, 1), (1, 0)])


def around(axis, values):
    return [
        lax.ppermute(values, axis, [(n, (n + step) % 4) for n in range(4)]) for step in (1, 2, 3)
    ]


def on_device(blocks, coords, live, factor_b, factor_c):
    block = blocks[0]
    coords = coords.reshape(3)
    full = (RANK, RANK)

    chunk, y = call(
        first_kernel,
        [pltpu.with_memory_space_constraint(v, pltpu.HBM) for v in (coords, block, factor_b, factor_c)],
        [(256, RANK), (BI, BJ, RANK)],
        "first",
        1,
        [
            pltpu.VMEM((BI, BJ, BK), BF16),
            pltpu.VMEM((BK, RANK), F32),
            pltpu.VMEM((BJ, RANK), F32),
            pltpu.VMEM((64, RANK), F32),
            pltpu.VMEM((64, RANK), F32),
            pltpu.SemaphoreType.DMA((8,)),
        ],
        pltpu.HBM,
    )
    got = exchange(chunk, ("ja", "ka"), 32, 8, RANK)
    spread, diagonal = call(collect_first_kernel, (got,), [(384, RANK), (8, RANK)], "collect_a")
    got = exchange(spread, ("ja", "ka"), 32, 3, 4, RANK)

    solved_a, gram_c, keep, send = call(
        second_kernel,
        (coords, got, diagonal, y),
        [(256, RANK), full, (104, RANK), (104, RANK)],
        "second",
        1,
        [pltpu.VMEM((BJ, RANK), F32), pltpu.VMEM(full, F32)],
    )
    parts, gram_half = call(
        merge_kernel, (keep, swap_cores(send)), [(72, RANK), (64, RANK)], "merge"
    )
    (half,) = call(
        dense_kernel,
        (parts, *around("ka", parts), gram_half),
        [(192, RANK)],
        "dense",
        0,
        [pltpu.VMEM((288, RANK), F32)],
    )
    (half,) = call(
        sum_kernel,
        (half, *around("iy", half)),
        [(192, RANK)],
        "sum",
        0,
        [pltpu.VMEM((768, RANK), F32)],
    )

    loading_a, solved_b, chunk, gram_a = call(
        third_kernel,
        (coords, half, swap_cores(half), gram_c, solved_a, block),
        [(256, RANK), (256, RANK), (256, RANK), full],
        "third",
        1,
        [pltpu.VMEM((BI * BJ, RANK), BF16), pltpu.VMEM((384, RANK), F32)],
    )
    got = exchange(chunk, (*IA, "ja"), 64, 4, RANK)
    (spread,) = call(collect_third_kernel, (got,), [(320, RANK)], "collect_c")
    same = exchange(spread, ("iy", "ja"), 32, 5, 2, RANK)
    other = swap_cores(same)

    loading_b, solved_c, squares = call(
        fourth_kernel,
        (same, other, gram_a, solved_b),
        [(256, RANK), (512, RANK), (1, RANK)],
        "fourth",
        0,
        [pltpu.VMEM((640, RANK), F32)],
    )
    total = squares + sum(around("ka", squares))
    loading_c = solved_c * lax.rsqrt(total / ROWS + EPSILON)
    return (loading_a, loading_b, loading_c)


def solution(mesh):
    shape = mesh.devices.shape
    split = jax.sharding.Mesh(
        mesh.devices.reshape(shape[0] // 2, 2, *shape[1:]), (*IA, "ja", "ka")
    )
    every = (*IA, "ja", "ka")
    placed = (P(every, None, None, None), P(None, every), P(every), P("ja", None), P("ka", None))
    return jax.shard_map(
        on_device,
        mesh=split,
        in_specs=placed,
        out_specs=(P(IA, None), P("ja", None), P("ka", None)),
        check_vma=False,
    )
```

```python
import jax
import jax.numpy as jnp
from jax import lax
from jax.experimental import pallas as pl
from jax.experimental.pallas import tpu as pltpu
from jax.sharding import PartitionSpec as P


RANK = 128
BI = 64
BJ = 64
BK = 128
SLOTS = 4
ROWS = 2048
IA = ("iy", "ic")

RIDGE_SHARE = 0.3
EPSILON = 1e-06
HIGHEST = lax.Precision.HIGHEST
F32 = jnp.float32
BF16 = jnp.bfloat16


def exact_dot(left, right):
    return jnp.dot(left, right, precision=HIGHEST, preferred_element_type=F32)


def across_rows(left, right):
    return lax.dot_general(
        left, right, (((0,), (0,)), ((), ())), precision=HIGHEST, preferred_element_type=F32
    )


def gram(rows):
    return across_rows(rows, rows)


def halves(values):
    high = values.astype(BF16)
    return high, (values - high.astype(F32)).astype(BF16)


def iotas():
    shape = (RANK, RANK)
    return lax.broadcasted_iota(jnp.int32, shape, 0), lax.broadcasted_iota(jnp.int32, shape, 1)


def inverse(matrix):
    count = RANK // 8
    rows = [matrix[8 * n : 8 * n + 8, :] for n in range(count)]
    lane = lax.broadcasted_iota(jnp.int32, (8, RANK), 1)
    sub = lax.broadcasted_iota(jnp.int32, (8, RANK), 0)
    one = jnp.clip(rows[0], 1.0, 1.0)
    lefts, rights = [], []

    def over_lanes(tile, at):
        return jnp.broadcast_to(tile[:, at : at + 1], (8, RANK))

    def over_rows(tile, at):
        return jnp.broadcast_to(tile[at : at + 1, :], (8, RANK))

    for k in range(count // 2):
        low = 16 * k
        inside = (lane >= low) & (lane < low + 16)
        unit = [jnp.where(lane - low - 8 * h == sub, 1.0, 0.0) for h in range(2)]
        panel = rows[2 * k : 2 * k + 2]
        lefts += [jnp.where(lane < low, panel[h], unit[h]) for h in range(2)]
        columns = [[over_lanes(panel[h], low + t) * one for h in range(2)] for t in range(16)]
        panel = [jnp.where(inside, unit[h], panel[h]) for h in range(2)]
        for s in range(16):
            h, q = divmod(s, 8)
            pivot = over_rows(1.0 / columns[s][h], q)
            keep = jnp.where(sub == q, pivot, 1.0)
            here = jnp.where(sub == q, 0.0, columns[s][h]) * pivot
            there = columns[s][1 - h] * pivot

            def eliminate(pair):
                lead = over_rows(pair[h], q)
                result = [pair[h] * keep - here * lead, pair[1 - h] - there * lead]
                return result if h == 0 else result[::-1]

            panel = eliminate(panel)
            for t in range(s + 1, 16):
                columns[t] = eliminate(columns[t])
        rights += [jnp.where(lane < low + 16, panel[h], 0.0) for h in range(2)]
        rows[2 * k : 2 * k + 2] = panel
        leads = [over_rows(panel[s // 8], s % 8) for s in range(16)]
        for n in range(2 * k + 2, count):
            terms = [over_lanes(rows[n], low + s) * leads[s] for s in range(16)]
            while len(terms) > 1:
                terms = [terms[i] + terms[i + 1] for i in range(0, len(terms), 2)]
            rows[n] = jnp.where(inside, 0.0, rows[n]) - terms[0]
    return across_rows(jnp.concatenate(lefts, axis=0), jnp.concatenate(rights, axis=0))


def system_inverse(merged):
    row, col = iotas()
    shift = jnp.sum(jnp.where(row == col, merged, 0.0)) * (RIDGE_SHARE / RANK)
    return inverse(merged + jnp.where(row == col, shift, 0.0))


def strided(ref, start, count, step):
    return ref[pl.ds(start, count, stride=step), :]


def put(ref, start, count, step, value):
    ref[pl.ds(start, count, stride=step), :] = value


def scaled_gram(raw):
    row, col = iotas()
    diagonal = jnp.where(row == col, raw, 0.0)
    across = lax.rsqrt(jnp.sum(diagonal, axis=0, keepdims=True) + EPSILON)
    down = lax.rsqrt(jnp.sum(diagonal, axis=1, keepdims=True) + EPSILON)
    return across, raw * down * across


def places(coords_ref):
    at = [lax.axis_index(IA), lax.axis_index("ja"), lax.axis_index("ka")]
    return at, [coords_ref[n] - 4 * at[n] for n in range(3)]


def some_rows(ref, index, size):
    return ref[pl.ds(pl.multiple_of(index * size, size), size), :]


def first_kernel(
    coords_in, block_ref, b_ref, c_ref, chunk_ref, y_ref,
    x_in, c_in, b_in, coords_ref, sems,
):

    parts = [pl.ds(n * (BI // 4), BI // 4) for n in range(4)]
    pairs = [(coords_in, coords_ref), (c_ref, c_in), (b_ref, b_in)]
    pairs += [(block_ref.at[part], x_in.at[part]) for part in parts]
    copies = [pltpu.make_async_copy(*pair, sems.at[n]) for n, pair in enumerate(pairs)]
    for copy in copies:
        copy.start()
    for copy in copies[:3]:
        copy.wait()
    at, slot = places(coords_ref)
    part_c = gram(some_rows(c_in, at[1], 64)) * (1.0 / ROWS)
    part_b = gram(some_rows(b_in, at[2], 64)) * (1.0 / ROWS)
    row, col = iotas()
    packed = jnp.where(row <= col, part_b, part_c)
    diagonal = jnp.sum(jnp.where(row == col, part_c, 0.0), axis=0, keepdims=True)
    for t in range(4):
        put(chunk_ref, 2 + t, 32, 8, packed[32 * t : 32 * t + 32])
    put(chunk_ref, 6, 32, 8, jnp.broadcast_to(diagonal, (32, RANK)))
    put(chunk_ref, 7, 32, 8, jnp.full((32, RANK), slot[0].astype(F32)))
    high, low = halves(some_rows(c_in, slot[2], BK))
    both = jnp.concatenate([high, low], axis=0)
    rows_b = some_rows(b_in, slot[1], BJ)
    partial = []
    for n, part in enumerate(parts):
        copies[3 + n].wait()
        block = x_in[part].reshape(BI // 4 * BJ, BK)
        y = jnp.dot(jnp.concatenate([block, block], axis=1), both, preferred_element_type=F32)
        y = y.reshape(BI // 4, BJ, RANK)
        y_ref[part] = y
        partial += [jnp.sum(y[m] * rows_b, axis=0, keepdims=True) for m in range(BI // 4)]
    for t in range(2):
        put(chunk_ref, t, 32, 8, jnp.concatenate(partial[32 * t : 32 * t + 32], axis=0))


def collect(got_ref, count, step, ids, extras):
    rows = []
    for slot in range(SLOTS):
        for t in range(2):
            picked = jnp.where(ids == slot, strided(got_ref, t, count, step), 0.0)
            rows.append(jnp.sum(picked, axis=0, keepdims=True))
    for t in range(extras):
        rows.append(jnp.sum(strided(got_ref, 2 + t, count, step), axis=0, keepdims=True))
    return rows


def lower_lanes(values):
    lane = lax.broadcasted_iota(jnp.int32, values.shape, 1)
    return jnp.where(lane < 64, values, pltpu.roll(values, 64, 1))


def mark(rows, slot):
    lane = lax.broadcasted_iota(jnp.int32, rows.shape, 1)
    return jnp.where(lane < 64, slot.astype(F32), rows)


def unmark(raw):
    row, col = iotas()
    return jnp.where((row >= 64) & (col < 64), raw.T, raw)


def repeat_rows(ref, rows, copies):
    width = len(rows)
    unit = 1
    while width * unit % 8:
        unit *= 2
    tile = jnp.concatenate(rows * unit, axis=0)
    for n in range(copies // unit):
        ref[n * width * unit : (n + 1) * width * unit, :] = tile


def collect_first_kernel(got_ref, spread_ref, diagonal_ref):
    rows = collect(got_ref, 32, 8, strided(got_ref, 7, 32, 8), 5)
    repeat_rows(spread_ref, rows[:12], 32)
    diagonal_ref[...] = jnp.broadcast_to(rows[12], (8, RANK))


def collect_third_kernel(got_ref, spread_ref):
    rows = collect(got_ref, 64, 4, lower_lanes(strided(got_ref, 3, 64, 4)), 2)
    repeat_rows(spread_ref, rows, 32)


def natural(got_ref, count, step, first, last):
    return jnp.concatenate([strided(got_ref, t, count, step) for t in range(first, last)], axis=0)


def second_kernel(
    coords_ref, got_ref, diagonal_ref, y_ref,
    solved_ref, gram_c_ref, keep_ref, send_ref, partial_ref, raw_ref,
):
    _, slot = places(coords_ref)
    packed = natural(got_ref, 32, 12, 8, 12)
    flipped = packed.T
    row, col = iotas()
    gram_b = jnp.where(row <= col, packed, flipped)
    gram_c = jnp.where(row < col, flipped, packed)
    gram_c = jnp.where(row == col, diagonal_ref[0:1, :], gram_c)
    gram_c_ref[...] = gram_c
    solver = system_inverse(gram_b * gram_c)
    solved = exact_dot(natural(got_ref, 32, 12, 0, 8), solver)
    solved_ref[...] = solved
    raw_ref[...] = gram(solved) * (1.0 / ROWS)
    own = some_rows(solved_ref, slot[0], BI)
    sums = [jnp.zeros((BJ, RANK), F32) for _ in range(2)]
    for n in range(BI):
        sums[n % 2] = sums[n % 2] + own[n : n + 1, :] * y_ref[n]
    partial_ref[...] = sums[0] + sums[1]
    core = lax.axis_index("ic")
    for ref, half in ((keep_ref, core), (send_ref, 1 - core)):
        ref[0:32, :] = some_rows(partial_ref, half, 32)
        ref[32:96, :] = some_rows(raw_ref, half, 64)
        ref[96:104, :] = jnp.full((8, RANK), slot[1].astype(F32))


def merge_kernel(keep_ref, other_ref, parts_ref, gram_ref):
    first = lax.broadcasted_iota(jnp.int32, (8, RANK), 0) == 0
    parts_ref[0:32, :] = keep_ref[0:32, :]
    parts_ref[32:64, :] = other_ref[0:32, :]
    parts_ref[64:72, :] = jnp.where(first, keep_ref[96:104, :], other_ref[96:104, :])
    gram_ref[...] = keep_ref[32:96, :] + other_ref[32:96, :]


def in_source_order(axis, refs, all_ref):
    size = refs[0].shape[0]
    me = lax.axis_index(axis)
    for step, ref in enumerate(refs):
        source = lax.rem(me + 4 - step, 4)
        all_ref[pl.ds(pl.multiple_of(source * size, 8), size), :] = ref[...]


def dense_kernel(parts_0, parts_1, parts_2, parts_3, half_ref, all_ref):
    in_source_order("ka", (parts_0, parts_1, parts_2, parts_3), all_ref)
    sums = [jnp.zeros((32, RANK), F32) for _ in range(SLOTS)]
    for n in range(4):
        for part in range(2):
            rows = all_ref[72 * n + 32 * part : 72 * n + 32 * part + 32, :]
            ids = all_ref[72 * n + 64 + part : 72 * n + 65 + part, :]
            for slot in range(SLOTS):
                sums[slot] = sums[slot] + jnp.where(ids == slot, rows, 0.0)
    for slot in range(SLOTS):
        half_ref[32 * slot : 32 * slot + 32, :] = sums[slot]


def sum_kernel(half_0, half_1, half_2, half_3, sum_ref, all_ref):
    in_source_order("iy", (half_0, half_1, half_2, half_3), all_ref)
    size = sum_ref.shape[0]
    parts = [all_ref[size * n : size * n + size, :] for n in range(4)]
    sum_ref[...] = (parts[0] + parts[1]) + (parts[2] + parts[3])


def second_inverse_kernel(
    same_ref, other_ref, gram_c_ref, solved_a_ref,
    solver_ref, gram_a_ref, scale_ref, loading_a_ref, raw_ref,
):
    core = lax.axis_index("ic")
    for ref, half in ((same_ref, core), (other_ref, 1 - core)):
        raw_ref[pl.ds(pl.multiple_of(64 * half, 64), 64), :] = ref[...]
    scale, gram_a = scaled_gram(raw_ref[...])
    gram_a_ref[...] = gram_a
    scale_ref[...] = jnp.broadcast_to(scale, (8, RANK))
    loading_a_ref[...] = solved_a_ref[...] * scale
    solver_ref[...] = system_inverse(gram_a * gram_c_ref[...])


def third_kernel(
    coords_ref, same_ref, other_ref, solver_ref, scale_ref, solved_a_ref, block_ref,
    solved_ref, chunk_ref, khatri_ref, rows_ref,
):
    at, slot = places(coords_ref)
    core = lax.axis_index("ic")
    for ref, half in ((same_ref, core), (other_ref, 1 - core)):
        for n in range(SLOTS):
            place = pl.multiple_of(64 * n + 32 * half, 32)
            rows_ref[pl.ds(place, 32), :] = ref[32 * n : 32 * n + 32, :]
    solved_ref[...] = exact_dot(rows_ref[...] * scale_ref[0:1, :], solver_ref[...])
    raw = gram(some_rows(solved_ref, at[0], 32)) * (1.0 / ROWS)
    own_a = some_rows(solved_a_ref, slot[0], BI) * scale_ref[0:1, :]
    own_b = some_rows(solved_ref, slot[1], BJ)
    for n in range(BI):
        khatri_ref[n * BJ : (n + 1) * BJ, :] = (own_a[n : n + 1, :] * own_b).astype(BF16)
    partial = lax.dot_general(
        block_ref[...].reshape(BI * BJ, BK),
        khatri_ref[...],
        (((0,), (0,)), ((), ())),
        preferred_element_type=F32,
    )
    for t in range(2):
        put(chunk_ref, t, 64, 4, partial[64 * t : 64 * t + 64])
    put(chunk_ref, 2, 64, 4, raw[0:64])
    put(chunk_ref, 3, 64, 4, mark(raw[64:128], slot[2]))


def fourth_kernel(
    same_ref, other_ref, gram_a_ref, solved_b_ref, loading_b_ref, solved_ref, squares_ref, rows_ref
):
    core = lax.axis_index("ic")
    for ref, half in ((same_ref, core), (other_ref, 1 - core)):
        for t in range(10):
            for n in range(4):
                place = pl.multiple_of(64 * t + 16 * n + 8 * half, 8)
                rows_ref[pl.ds(place, 8), :] = strided(ref, 80 * n + t, 8, 10)
    scale, gram_b = scaled_gram(unmark(rows_ref[512:640, :]))
    loading_b_ref[...] = solved_b_ref[...] * scale
    solver = system_inverse(gram_a_ref[...] * gram_b)
    solved = exact_dot(rows_ref[0:512, :] * scale, solver)
    solved_ref[...] = solved
    squares_ref[...] = jnp.sum(solved * solved, axis=0, keepdims=True)


def call(kernel, operands, outs, scalars=0, scratch=(), space=pltpu.VMEM):
    vmem = pl.BlockSpec(memory_space=pltpu.VMEM)
    smem = pl.BlockSpec(memory_space=pltpu.SMEM)
    return pl.pallas_call(
        kernel,
        out_shape=[jax.ShapeDtypeStruct(shape, F32) for shape in outs],
        in_specs=[smem] * scalars + [pl.BlockSpec(memory_space=space)] * (len(operands) - scalars),
        out_specs=[vmem] * len(outs),
        scratch_shapes=scratch,
        compiler_params=pltpu.CompilerParams(vmem_limit_bytes=32 << 20),
    )(*operands)


def exchange(values, axes, *chunk):
    shape = values.shape
    return lax.all_to_all(values.reshape(chunk), axes, 0, 0, tiled=True).reshape(shape)


def swap_cores(values):
    return lax.ppermute(values, "ic", [(0, 1), (1, 0)])


def around(axis, values):
    return [
        lax.ppermute(values, axis, [(n, (n + step) % 4) for n in range(4)]) for step in (1, 2, 3)
    ]


def on_device(blocks, coords, live, factor_b, factor_c):
    block = blocks[0]
    coords = coords.reshape(3)
    full = (RANK, RANK)

    chunk, y = call(
        first_kernel,
        [pltpu.with_memory_space_constraint(v, pltpu.HBM) for v in (coords, block, factor_b, factor_c)],
        [(256, RANK), (BI, BJ, RANK)],
        0,
        [
            pltpu.VMEM((BI, BJ, BK), BF16),
            pltpu.VMEM((512, RANK), F32),
            pltpu.VMEM((256, RANK), F32),
            pltpu.SMEM((3,), jnp.int32),
            pltpu.SemaphoreType.DMA((7,)),
        ],
        pltpu.HBM,
    )
    got = exchange(chunk, ("ja", "ka"), 32, 8, RANK)
    spread, diagonal = call(collect_first_kernel, (got,), [(384, RANK), (8, RANK)])
    got = exchange(spread, ("ja", "ka"), 32, 3, 4, RANK)

    solved_a, gram_c, keep, send = call(
        second_kernel,
        (coords, got, diagonal, y),
        [(256, RANK), full, (104, RANK), (104, RANK)],
        1,
        [pltpu.VMEM((BJ, RANK), F32), pltpu.VMEM(full, F32)],
    )
    parts, gram_half = call(merge_kernel, (keep, swap_cores(send)), [(72, RANK), (64, RANK)])
    around_x = around("ka", parts)
    (gram_half,) = call(
        sum_kernel,
        (gram_half, *around("iy", gram_half)),
        [(64, RANK)],
        0,
        [pltpu.VMEM((256, RANK), F32)],
    )
    (half,) = call(dense_kernel, (parts, *around_x), [full], 0, [pltpu.VMEM((288, RANK), F32)])
    other = swap_cores(gram_half)
    around_y = around("iy", half)
    solver, gram_a, scale, loading_a = call(
        second_inverse_kernel,
        (gram_half, other, gram_c, solved_a),
        [full, full, (8, RANK), (256, RANK)],
        0,
        [pltpu.VMEM(full, F32)],
    )
    (half,) = call(sum_kernel, (half, *around_y), [full], 0, [pltpu.VMEM((512, RANK), F32)])

    solved_b, chunk = call(
        third_kernel,
        (coords, half, swap_cores(half), solver, scale, solved_a, block),
        [(256, RANK), (256, RANK)],
        1,
        [pltpu.VMEM((BI * BJ, RANK), BF16), pltpu.VMEM((256, RANK), F32)],
    )
    got = exchange(chunk, (*IA, "ja"), 64, 4, RANK)
    (spread,) = call(collect_third_kernel, (got,), [(320, RANK)])
    same = exchange(spread, ("iy", "ja"), 32, 5, 2, RANK)
    other = swap_cores(same)

    loading_b, solved_c, squares = call(
        fourth_kernel,
        (same, other, gram_a, solved_b),
        [(256, RANK), (512, RANK), (1, RANK)],
        0,
        [pltpu.VMEM((640, RANK), F32)],
    )
    total = squares + sum(around("ka", squares))
    loading_c = solved_c * lax.rsqrt(total / ROWS + EPSILON)
    return (loading_a, loading_b, loading_c)


def solution(mesh):
    shape = mesh.devices.shape
    split = jax.sharding.Mesh(
        mesh.devices.reshape(shape[0] // 2, 2, *shape[1:]), (*IA, "ja", "ka")
    )
    every = (*IA, "ja", "ka")
    placed = (P(every, None, None, None), P(None, every), P(every), P("ja", None), P("ka", None))
    return jax.shard_map(
        on_device,
        mesh=split,
        in_specs=placed,
        out_specs=(P(IA, None), P("ja", None), P("ka", None)),
        check_vma=False,
    )
```

```python
import jax
import jax.numpy as jnp
from jax import lax
from jax.experimental import pallas as pl
from jax.experimental.pallas import tpu as pltpu
from jax.sharding import PartitionSpec as P


RANK = 128
BI = 64
BJ = 64
BK = 128
SLOTS = 4
ROWS = 2048
IA = ("iy", "ic")

RIDGE_SHARE = 0.3
EPSILON = 1e-06
HIGHEST = lax.Precision.HIGHEST
F32 = jnp.float32
BF16 = jnp.bfloat16


def exact_dot(left, right):
    return jnp.dot(left, right, precision=HIGHEST, preferred_element_type=F32)


def across_rows(left, right):
    return lax.dot_general(
        left, right, (((0,), (0,)), ((), ())), precision=HIGHEST, preferred_element_type=F32
    )


def gram(rows):
    return across_rows(rows, rows)


def halves(values):
    high = values.astype(BF16)
    return high, (values - high.astype(F32)).astype(BF16)


def iotas():
    shape = (RANK, RANK)
    return lax.broadcasted_iota(jnp.int32, shape, 0), lax.broadcasted_iota(jnp.int32, shape, 1)


def inverse(matrix):
    count = RANK // 8
    rows = [matrix[8 * n : 8 * n + 8, :] for n in range(count)]
    lane = lax.broadcasted_iota(jnp.int32, (8, RANK), 1)
    sub = lax.broadcasted_iota(jnp.int32, (8, RANK), 0)
    one = jnp.clip(rows[0], 1.0, 1.0)
    lefts, rights = [], []

    def over_lanes(tile, at):
        return jnp.broadcast_to(tile[:, at : at + 1], (8, RANK))

    def over_rows(tile, at):
        return jnp.broadcast_to(tile[at : at + 1, :], (8, RANK))

    for k in range(count // 2):
        low = 16 * k
        inside = (lane >= low) & (lane < low + 16)
        unit = [jnp.where(lane - low - 8 * h == sub, 1.0, 0.0) for h in range(2)]
        panel = rows[2 * k : 2 * k + 2]
        lefts += [jnp.where(lane < low, panel[h], unit[h]) for h in range(2)]
        columns = [[over_lanes(panel[h], low + t) * one for h in range(2)] for t in range(16)]
        panel = [jnp.where(inside, unit[h], panel[h]) for h in range(2)]
        for s in range(16):
            h, q = divmod(s, 8)
            pivot = over_rows(1.0 / columns[s][h], q)
            keep = jnp.where(sub == q, pivot, 1.0)
            here = jnp.where(sub == q, 0.0, columns[s][h]) * pivot
            there = columns[s][1 - h] * pivot

            def eliminate(pair):
                lead = over_rows(pair[h], q)
                result = [pair[h] * keep - here * lead, pair[1 - h] - there * lead]
                return result if h == 0 else result[::-1]

            panel = eliminate(panel)
            for t in range(s + 1, 16):
                columns[t] = eliminate(columns[t])
        rights += [jnp.where(lane < low + 16, panel[h], 0.0) for h in range(2)]
        rows[2 * k : 2 * k + 2] = panel
        leads = [over_rows(panel[s // 8], s % 8) for s in range(16)]
        for n in range(2 * k + 2, min(2 * k + 4, count)):
            terms = [over_lanes(rows[n], low + s) * leads[s] for s in range(16)]
            while len(terms) > 1:
                terms = [terms[i] + terms[i + 1] for i in range(0, len(terms), 2)]
            rows[n] = jnp.where(inside, 0.0, rows[n]) - terms[0]
        if 2 * k + 4 < count:
            later = jnp.concatenate(rows[2 * k + 4 :], axis=0)
            update = exact_dot(later[:, low : low + 16], jnp.concatenate(panel, axis=0))
            for m, n in enumerate(range(2 * k + 4, count)):
                rows[n] = jnp.where(inside, 0.0, rows[n]) - update[8 * m : 8 * m + 8]
    return across_rows(jnp.concatenate(lefts, axis=0), jnp.concatenate(rights, axis=0))


def system_inverse(merged):
    row, col = iotas()
    shift = jnp.sum(jnp.where(row == col, merged, 0.0)) * (RIDGE_SHARE / RANK)
    return inverse(merged + jnp.where(row == col, shift, 0.0))


def strided(ref, start, count, step):
    return ref[pl.ds(start, count, stride=step), :]


def put(ref, start, count, step, value):
    ref[pl.ds(start, count, stride=step), :] = value


def scaled_gram(raw):
    row, col = iotas()
    diagonal = jnp.where(row == col, raw, 0.0)
    across = lax.rsqrt(jnp.sum(diagonal, axis=0, keepdims=True) + EPSILON)
    down = lax.rsqrt(jnp.sum(diagonal, axis=1, keepdims=True) + EPSILON)
    return across, raw * down * across


def places(coords_ref):
    at = [lax.axis_index(IA), lax.axis_index("ja"), lax.axis_index("ka")]
    return at, [coords_ref[n] - 4 * at[n] for n in range(3)]


def some_rows(ref, index, size):
    return ref[pl.ds(pl.multiple_of(index * size, size), size), :]


def first_kernel(
    coords_in, block_ref, b_ref, c_ref, chunk_ref, y_ref,
    x_in, c_in, b_in, coords_ref, sems,
):

    parts = [pl.ds(n * (BI // 4), BI // 4) for n in range(4)]
    pairs = [(coords_in, coords_ref), (c_ref, c_in), (b_ref, b_in)]
    pairs += [(block_ref.at[part], x_in.at[part]) for part in parts]
    copies = [pltpu.make_async_copy(*pair, sems.at[n]) for n, pair in enumerate(pairs)]
    for copy in copies:
        copy.start()
    for copy in copies[:3]:
        copy.wait()
    at, slot = places(coords_ref)
    part_c = gram(some_rows(c_in, at[1], 64)) * (1.0 / ROWS)
    part_b = gram(some_rows(b_in, at[2], 64)) * (1.0 / ROWS)
    row, col = iotas()
    packed = jnp.where(row <= col, part_b, part_c)
    diagonal = jnp.sum(jnp.where(row == col, part_c, 0.0), axis=0, keepdims=True)
    for t in range(4):
        put(chunk_ref, 2 + t, 32, 8, packed[32 * t : 32 * t + 32])
    put(chunk_ref, 6, 32, 8, jnp.broadcast_to(diagonal, (32, RANK)))
    put(chunk_ref, 7, 32, 8, jnp.full((32, RANK), slot[0].astype(F32)))
    high, low = halves(some_rows(c_in, slot[2], BK))
    both = jnp.concatenate([high, low], axis=0)
    rows_b = some_rows(b_in, slot[1], BJ)
    partial = []
    for n, part in enumerate(parts):
        copies[3 + n].wait()
        block = x_in[part].reshape(BI // 4 * BJ, BK)
        y = jnp.dot(jnp.concatenate([block, block], axis=1), both, preferred_element_type=F32)
        y = y.reshape(BI // 4, BJ, RANK)
        y_ref[part] = y
        partial += [jnp.sum(y[m] * rows_b, axis=0, keepdims=True) for m in range(BI // 4)]
    for t in range(2):
        put(chunk_ref, t, 32, 8, jnp.concatenate(partial[32 * t : 32 * t + 32], axis=0))


def collect(got_ref, count, step, ids, extras):
    rows = []
    for slot in range(SLOTS):
        for t in range(2):
            picked = jnp.where(ids == slot, strided(got_ref, t, count, step), 0.0)
            rows.append(jnp.sum(picked, axis=0, keepdims=True))
    for t in range(extras):
        rows.append(jnp.sum(strided(got_ref, 2 + t, count, step), axis=0, keepdims=True))
    return rows


def lower_lanes(values):
    lane = lax.broadcasted_iota(jnp.int32, values.shape, 1)
    return jnp.where(lane < 64, values, pltpu.roll(values, 64, 1))


def mark(rows, slot):
    lane = lax.broadcasted_iota(jnp.int32, rows.shape, 1)
    return jnp.where(lane < 64, slot.astype(F32), rows)


def unmark(raw):
    row, col = iotas()
    return jnp.where((row >= 64) & (col < 64), raw.T, raw)


def repeat_rows(ref, rows, copies):
    width = len(rows)
    unit = 1
    while width * unit % 8:
        unit *= 2
    tile = jnp.concatenate(rows * unit, axis=0)
    for n in range(copies // unit):
        ref[n * width * unit : (n + 1) * width * unit, :] = tile


def collect_first_kernel(got_ref, spread_ref, diagonal_ref):
    rows = collect(got_ref, 32, 8, strided(got_ref, 7, 32, 8), 5)
    repeat_rows(spread_ref, rows[:12], 32)
    diagonal_ref[...] = jnp.broadcast_to(rows[12], (8, RANK))


def collect_third_kernel(got_ref, spread_ref):
    rows = collect(got_ref, 64, 4, lower_lanes(strided(got_ref, 3, 64, 4)), 2)
    repeat_rows(spread_ref, rows, 32)


def natural(got_ref, count, step, first, last):
    return jnp.concatenate([strided(got_ref, t, count, step) for t in range(first, last)], axis=0)


def second_kernel(
    coords_ref, got_ref, diagonal_ref, y_ref,
    solved_ref, gram_c_ref, keep_ref, send_ref, partial_ref, raw_ref,
):
    _, slot = places(coords_ref)
    packed = natural(got_ref, 32, 12, 8, 12)
    flipped = packed.T
    row, col = iotas()
    gram_b = jnp.where(row <= col, packed, flipped)
    gram_c = jnp.where(row < col, flipped, packed)
    gram_c = jnp.where(row == col, diagonal_ref[0:1, :], gram_c)
    gram_c_ref[...] = gram_c
    solver = system_inverse(gram_b * gram_c)
    solved = exact_dot(natural(got_ref, 32, 12, 0, 8), solver)
    solved_ref[...] = solved
    raw_ref[...] = gram(solved) * (1.0 / ROWS)
    own = some_rows(solved_ref, slot[0], BI)
    sums = [jnp.zeros((BJ, RANK), F32) for _ in range(2)]
    for n in range(BI):
        sums[n % 2] = sums[n % 2] + own[n : n + 1, :] * y_ref[n]
    partial_ref[...] = sums[0] + sums[1]
    core = lax.axis_index("ic")
    for ref, half in ((keep_ref, core), (send_ref, 1 - core)):
        ref[0:32, :] = some_rows(partial_ref, half, 32)
        ref[32:96, :] = some_rows(raw_ref, half, 64)
        ref[96:104, :] = jnp.full((8, RANK), slot[1].astype(F32))


def merge_kernel(keep_ref, other_ref, parts_ref, gram_ref):
    first = lax.broadcasted_iota(jnp.int32, (8, RANK), 0) == 0
    parts_ref[0:32, :] = keep_ref[0:32, :]
    parts_ref[32:64, :] = other_ref[0:32, :]
    parts_ref[64:72, :] = jnp.where(first, keep_ref[96:104, :], other_ref[96:104, :])
    gram_ref[...] = keep_ref[32:96, :] + other_ref[32:96, :]


def in_source_order(axis, refs, all_ref):
    size = refs[0].shape[0]
    me = lax.axis_index(axis)
    for step, ref in enumerate(refs):
        source = lax.rem(me + 4 - step, 4)
        all_ref[pl.ds(pl.multiple_of(source * size, 8), size), :] = ref[...]


def dense_kernel(parts_0, parts_1, parts_2, parts_3, half_ref, all_ref):
    in_source_order("ka", (parts_0, parts_1, parts_2, parts_3), all_ref)
    sums = [jnp.zeros((32, RANK), F32) for _ in range(SLOTS)]
    for n in range(4):
        for part in range(2):
            rows = all_ref[72 * n + 32 * part : 72 * n + 32 * part + 32, :]
            ids = all_ref[72 * n + 64 + part : 72 * n + 65 + part, :]
            for slot in range(SLOTS):
                sums[slot] = sums[slot] + jnp.where(ids == slot, rows, 0.0)
    for slot in range(SLOTS):
        half_ref[32 * slot : 32 * slot + 32, :] = sums[slot]


def sum_kernel(half_0, half_1, half_2, half_3, sum_ref, all_ref):
    in_source_order("iy", (half_0, half_1, half_2, half_3), all_ref)
    size = sum_ref.shape[0]
    parts = [all_ref[size * n : size * n + size, :] for n in range(4)]
    sum_ref[...] = (parts[0] + parts[1]) + (parts[2] + parts[3])


def second_inverse_kernel(
    same_ref, other_ref, gram_c_ref, solved_a_ref,
    solver_ref, gram_a_ref, scale_ref, loading_a_ref, raw_ref,
):
    core = lax.axis_index("ic")
    for ref, half in ((same_ref, core), (other_ref, 1 - core)):
        raw_ref[pl.ds(pl.multiple_of(64 * half, 64), 64), :] = ref[...]
    scale, gram_a = scaled_gram(raw_ref[...])
    gram_a_ref[...] = gram_a
    scale_ref[...] = jnp.broadcast_to(scale, (8, RANK))
    loading_a_ref[...] = solved_a_ref[...] * scale
    solver_ref[...] = system_inverse(gram_a * gram_c_ref[...])


def third_kernel(
    coords_ref, same_ref, other_ref, solver_ref, scale_ref, solved_a_ref, block_ref,
    solved_ref, chunk_ref, khatri_ref, rows_ref,
):
    at, slot = places(coords_ref)
    core = lax.axis_index("ic")
    for ref, half in ((same_ref, core), (other_ref, 1 - core)):
        for n in range(SLOTS):
            place = pl.multiple_of(64 * n + 32 * half, 32)
            rows_ref[pl.ds(place, 32), :] = ref[32 * n : 32 * n + 32, :]
    solved_ref[...] = exact_dot(rows_ref[...] * scale_ref[0:1, :], solver_ref[...])
    raw = gram(some_rows(solved_ref, at[0], 32)) * (1.0 / ROWS)
    own_a = some_rows(solved_a_ref, slot[0], BI) * scale_ref[0:1, :]
    own_b = some_rows(solved_ref, slot[1], BJ)
    for n in range(BI):
        khatri_ref[n * BJ : (n + 1) * BJ, :] = (own_a[n : n + 1, :] * own_b).astype(BF16)
    partial = lax.dot_general(
        block_ref[...].reshape(BI * BJ, BK),
        khatri_ref[...],
        (((0,), (0,)), ((), ())),
        preferred_element_type=F32,
    )
    for t in range(2):
        put(chunk_ref, t, 64, 4, partial[64 * t : 64 * t + 64])
    put(chunk_ref, 2, 64, 4, raw[0:64])
    put(chunk_ref, 3, 64, 4, mark(raw[64:128], slot[2]))


def fourth_kernel(
    same_ref, other_ref, gram_a_ref, solved_b_ref, loading_b_ref, solved_ref, squares_ref, rows_ref
):
    core = lax.axis_index("ic")
    for ref, half in ((same_ref, core), (other_ref, 1 - core)):
        for t in range(10):
            for n in range(4):
                place = pl.multiple_of(64 * t + 16 * n + 8 * half, 8)
                rows_ref[pl.ds(place, 8), :] = strided(ref, 80 * n + t, 8, 10)
    scale, gram_b = scaled_gram(unmark(rows_ref[512:640, :]))
    loading_b_ref[...] = solved_b_ref[...] * scale
    solver = system_inverse(gram_a_ref[...] * gram_b)
    solved = exact_dot(rows_ref[0:512, :] * scale, solver)
    solved_ref[...] = solved
    squares_ref[...] = jnp.sum(solved * solved, axis=0, keepdims=True)


def call(kernel, operands, outs, scalars=0, scratch=(), space=pltpu.VMEM):
    vmem = pl.BlockSpec(memory_space=pltpu.VMEM)
    smem = pl.BlockSpec(memory_space=pltpu.SMEM)
    return pl.pallas_call(
        kernel,
        out_shape=[jax.ShapeDtypeStruct(shape, F32) for shape in outs],
        in_specs=[smem] * scalars + [pl.BlockSpec(memory_space=space)] * (len(operands) - scalars),
        out_specs=[vmem] * len(outs),
        scratch_shapes=scratch,
        compiler_params=pltpu.CompilerParams(vmem_limit_bytes=32 << 20),
    )(*operands)


def exchange(values, axes, *chunk):
    shape = values.shape
    return lax.all_to_all(values.reshape(chunk), axes, 0, 0, tiled=True).reshape(shape)


def swap_cores(values):
    return lax.ppermute(values, "ic", [(0, 1), (1, 0)])


def around(axis, values):
    return [
        lax.ppermute(values, axis, [(n, (n + step) % 4) for n in range(4)]) for step in (1, 2, 3)
    ]


def on_device(blocks, coords, live, factor_b, factor_c):
    block = blocks[0]
    coords = coords.reshape(3)
    full = (RANK, RANK)

    chunk, y = call(
        first_kernel,
        [pltpu.with_memory_space_constraint(v, pltpu.HBM) for v in (coords, block, factor_b, factor_c)],
        [(256, RANK), (BI, BJ, RANK)],
        0,
        [
            pltpu.VMEM((BI, BJ, BK), BF16),
            pltpu.VMEM((512, RANK), F32),
            pltpu.VMEM((256, RANK), F32),
            pltpu.SMEM((3,), jnp.int32),
            pltpu.SemaphoreType.DMA((7,)),
        ],
        pltpu.HBM,
    )
    got = exchange(chunk, ("ja", "ka"), 32, 8, RANK)
    spread, diagonal = call(collect_first_kernel, (got,), [(384, RANK), (8, RANK)])
    got = exchange(spread, ("ja", "ka"), 32, 3, 4, RANK)

    solved_a, gram_c, keep, send = call(
        second_kernel,
        (coords, got, diagonal, y),
        [(256, RANK), full, (104, RANK), (104, RANK)],
        1,
        [pltpu.VMEM((BJ, RANK), F32), pltpu.VMEM(full, F32)],
    )
    parts, gram_half = call(merge_kernel, (keep, swap_cores(send)), [(72, RANK), (64, RANK)])
    around_x = around("ka", parts)
    (gram_half,) = call(
        sum_kernel,
        (gram_half, *around("iy", gram_half)),
        [(64, RANK)],
        0,
        [pltpu.VMEM((256, RANK), F32)],
    )
    (half,) = call(dense_kernel, (parts, *around_x), [full], 0, [pltpu.VMEM((288, RANK), F32)])
    other = swap_cores(gram_half)
    around_y = around("iy", half)
    solver, gram_a, scale, loading_a = call(
        second_inverse_kernel,
        (gram_half, other, gram_c, solved_a),
        [full, full, (8, RANK), (256, RANK)],
        0,
        [pltpu.VMEM(full, F32)],
    )
    (half,) = call(sum_kernel, (half, *around_y), [full], 0, [pltpu.VMEM((512, RANK), F32)])

    solved_b, chunk = call(
        third_kernel,
        (coords, half, swap_cores(half), solver, scale, solved_a, block),
        [(256, RANK), (256, RANK)],
        1,
        [pltpu.VMEM((BI * BJ, RANK), BF16), pltpu.VMEM((256, RANK), F32)],
    )
    got = exchange(chunk, (*IA, "ja"), 64, 4, RANK)
    (spread,) = call(collect_third_kernel, (got,), [(320, RANK)])
    same = exchange(spread, ("iy", "ja"), 32, 5, 2, RANK)
    other = swap_cores(same)

    loading_b, solved_c, squares = call(
        fourth_kernel,
        (same, other, gram_a, solved_b),
        [(256, RANK), (512, RANK), (1, RANK)],
        0,
        [pltpu.VMEM((640, RANK), F32)],
    )
    total = squares + sum(around("ka", squares))
    loading_c = solved_c * lax.rsqrt(total / ROWS + EPSILON)
    return (loading_a, loading_b, loading_c)


def solution(mesh):
    shape = mesh.devices.shape
    split = jax.sharding.Mesh(
        mesh.devices.reshape(shape[0] // 2, 2, *shape[1:]), (*IA, "ja", "ka")
    )
    every = (*IA, "ja", "ka")
    placed = (P(every, None, None, None), P(None, every), P(every), P("ja", None), P("ka", None))
    return jax.shard_map(
        on_device,
        mesh=split,
        in_specs=placed,
        out_specs=(P(IA, None), P("ja", None), P("ka", None)),
        check_vma=False,
    )
```

```python
import jax
import jax.numpy as jnp
from jax import lax
from jax.experimental import pallas as pl
from jax.experimental.pallas import tpu as pltpu
from jax.sharding import PartitionSpec as P


RANK = 128
BI = 64
BJ = 64
BK = 128
SLOTS = 4
ROWS = 2048
IA = ("iy", "ic")

RIDGE_SHARE = 0.3
EPSILON = 1e-06
HIGHEST = lax.Precision.HIGHEST
F32 = jnp.float32
BF16 = jnp.bfloat16


def exact_dot(left, right):
    return jnp.dot(left, right, precision=HIGHEST, preferred_element_type=F32)


def across_rows(left, right):
    return lax.dot_general(
        left, right, (((0,), (0,)), ((), ())), precision=HIGHEST, preferred_element_type=F32
    )


def gram(rows):
    return across_rows(rows, rows)


def halves(values):
    high = values.astype(BF16)
    return high, (values - high.astype(F32)).astype(BF16)


def iotas():
    shape = (RANK, RANK)
    return lax.broadcasted_iota(jnp.int32, shape, 0), lax.broadcasted_iota(jnp.int32, shape, 1)


def inverse(matrix):
    count = RANK // 8
    rows = [matrix[8 * n : 8 * n + 8, :] for n in range(count)]
    lane = lax.broadcasted_iota(jnp.int32, (8, RANK), 1)
    sub = lax.broadcasted_iota(jnp.int32, (8, RANK), 0)
    one = jnp.clip(rows[0], 1.0, 1.0)
    lefts, rights = [], []

    def over_lanes(tile, at):
        return jnp.broadcast_to(tile[:, at : at + 1], (8, RANK))

    def over_rows(tile, at):
        return jnp.broadcast_to(tile[at : at + 1, :], (8, RANK))

    for k in range(count // 2):
        low = 16 * k
        inside = (lane >= low) & (lane < low + 16)
        unit = [jnp.where(lane - low - 8 * h == sub, 1.0, 0.0) for h in range(2)]
        panel = rows[2 * k : 2 * k + 2]
        lefts += [jnp.where(lane < low, panel[h], unit[h]) for h in range(2)]
        columns = [[over_lanes(panel[h], low + t) * one for h in range(2)] for t in range(16)]
        panel = [jnp.where(inside, unit[h], panel[h]) for h in range(2)]
        for s in range(16):
            h, q = divmod(s, 8)
            pivot = over_rows(1.0 / columns[s][h], q)
            keep = jnp.where(sub == q, pivot, 1.0)
            here = jnp.where(sub == q, 0.0, columns[s][h]) * pivot
            there = columns[s][1 - h] * pivot

            def eliminate(pair):
                lead = over_rows(pair[h], q)
                result = [pair[h] * keep - here * lead, pair[1 - h] - there * lead]
                return result if h == 0 else result[::-1]

            panel = eliminate(panel)
            for t in range(s + 1, 16):
                columns[t] = eliminate(columns[t])
        rights += [jnp.where(lane < low + 16, panel[h], 0.0) for h in range(2)]
        rows[2 * k : 2 * k + 2] = panel
        leads = [over_rows(panel[s // 8], s % 8) for s in range(16)]
        for n in range(2 * k + 2, min(2 * k + 4, count)):
            terms = [over_lanes(rows[n], low + s) * leads[s] for s in range(16)]
            while len(terms) > 1:
                terms = [terms[i] + terms[i + 1] for i in range(0, len(terms), 2)]
            rows[n] = jnp.where(inside, 0.0, rows[n]) - terms[0]
        if 2 * k + 4 < count:
            later = jnp.concatenate(rows[2 * k + 4 :], axis=0)
            update = exact_dot(later[:, low : low + 16], jnp.concatenate(panel, axis=0))
            for m, n in enumerate(range(2 * k + 4, count)):
                rows[n] = jnp.where(inside, 0.0, rows[n]) - update[8 * m : 8 * m + 8]
    return across_rows(jnp.concatenate(lefts, axis=0), jnp.concatenate(rights, axis=0))


def system_inverse(merged):
    row, col = iotas()
    shift = jnp.sum(jnp.where(row == col, merged, 0.0)) * (RIDGE_SHARE / RANK)
    return inverse(merged + jnp.where(row == col, shift, 0.0))


def strided(ref, start, count, step):
    return ref[pl.ds(start, count, stride=step), :]


def put(ref, start, count, step, value):
    ref[pl.ds(start, count, stride=step), :] = value


def scaled_gram(raw):
    row, col = iotas()
    diagonal = jnp.where(row == col, raw, 0.0)
    across = lax.rsqrt(jnp.sum(diagonal, axis=0, keepdims=True) + EPSILON)
    down = lax.rsqrt(jnp.sum(diagonal, axis=1, keepdims=True) + EPSILON)
    return across, raw * down * across


def places(coords_ref):
    at = [lax.axis_index(IA), lax.axis_index("ja"), lax.axis_index("ka")]
    return at, [coords_ref[n] - 4 * at[n] for n in range(3)]


def some_rows(ref, index, size):
    return ref[pl.ds(pl.multiple_of(index * size, size), size), :]


def first_kernel(
    coords_in, block_ref, b_ref, c_ref, chunk_ref, y_ref,
    x_in, c_in, b_in, coords_ref, sems,
):

    parts = [pl.ds(n * (BI // 4), BI // 4) for n in range(4)]
    pairs = [(coords_in, coords_ref), (c_ref, c_in), (b_ref, b_in)]
    pairs += [(block_ref.at[part], x_in.at[part]) for part in parts]
    copies = [pltpu.make_async_copy(*pair, sems.at[n]) for n, pair in enumerate(pairs)]
    for copy in copies:
        copy.start()
    for copy in copies[:3]:
        copy.wait()
    at, slot = places(coords_ref)
    part_c = gram(some_rows(c_in, at[1], 64)) * (1.0 / ROWS)
    part_b = gram(some_rows(b_in, at[2], 64)) * (1.0 / ROWS)
    row, col = iotas()
    packed = jnp.where(row <= col, part_b, part_c)
    diagonal = jnp.sum(jnp.where(row == col, part_c, 0.0), axis=0, keepdims=True)
    for t in range(4):
        put(chunk_ref, 2 + t, 32, 8, packed[32 * t : 32 * t + 32])
    put(chunk_ref, 6, 32, 8, jnp.broadcast_to(diagonal, (32, RANK)))
    put(chunk_ref, 7, 32, 8, jnp.full((32, RANK), slot[0].astype(F32)))
    high, low = halves(some_rows(c_in, slot[2], BK))
    both = jnp.concatenate([high, low], axis=0)
    rows_b = some_rows(b_in, slot[1], BJ)
    partial = []
    for n, part in enumerate(parts):
        copies[3 + n].wait()
        block = x_in[part].reshape(BI // 4 * BJ, BK)
        y = jnp.dot(jnp.concatenate([block, block], axis=1), both, preferred_element_type=F32)
        y = y.reshape(BI // 4, BJ, RANK)
        y_ref[part] = y
        partial += [jnp.sum(y[m] * rows_b, axis=0, keepdims=True) for m in range(BI // 4)]
    for t in range(2):
        put(chunk_ref, t, 32, 8, jnp.concatenate(partial[32 * t : 32 * t + 32], axis=0))


def collect(got_ref, count, step, ids, extras):
    rows = []
    for slot in range(SLOTS):
        for t in range(2):
            picked = jnp.where(ids == slot, strided(got_ref, t, count, step), 0.0)
            rows.append(jnp.sum(picked, axis=0, keepdims=True))
    for t in range(extras):
        rows.append(jnp.sum(strided(got_ref, 2 + t, count, step), axis=0, keepdims=True))
    return rows


def lower_lanes(values):
    lane = lax.broadcasted_iota(jnp.int32, values.shape, 1)
    return jnp.where(lane < 64, values, pltpu.roll(values, 64, 1))


def mark(rows, slot):
    lane = lax.broadcasted_iota(jnp.int32, rows.shape, 1)
    return jnp.where(lane < 64, slot.astype(F32), rows)


def unmark(raw):
    row, col = iotas()
    return jnp.where((row >= 64) & (col < 64), raw.T, raw)


def repeat_rows(ref, rows, copies):
    width = len(rows)
    unit = 1
    while width * unit % 8:
        unit *= 2
    tile = jnp.concatenate(rows * unit, axis=0)
    for n in range(copies // unit):
        ref[n * width * unit : (n + 1) * width * unit, :] = tile


def collect_first_kernel(got_ref, spread_ref, diagonal_ref):
    rows = collect(got_ref, 32, 8, strided(got_ref, 7, 32, 8), 5)
    repeat_rows(spread_ref, rows[:12], 32)
    diagonal_ref[...] = jnp.broadcast_to(rows[12], (8, RANK))


def collect_third_kernel(got_ref, spread_ref):
    rows = collect(got_ref, 64, 4, lower_lanes(strided(got_ref, 3, 64, 4)), 2)
    repeat_rows(spread_ref, rows, 32)


def natural(got_ref, count, step, first, last):
    return jnp.concatenate([strided(got_ref, t, count, step) for t in range(first, last)], axis=0)


def second_kernel(
    coords_ref, got_ref, diagonal_ref, y_ref,
    solved_ref, gram_c_ref, keep_ref, send_ref, partial_ref, raw_ref,
):
    _, slot = places(coords_ref)
    packed = natural(got_ref, 32, 12, 8, 12)
    flipped = packed.T
    row, col = iotas()
    gram_b = jnp.where(row <= col, packed, flipped)
    gram_c = jnp.where(row < col, flipped, packed)
    gram_c = jnp.where(row == col, diagonal_ref[0:1, :], gram_c)
    gram_c_ref[...] = gram_c
    solver = system_inverse(gram_b * gram_c)
    solved = exact_dot(natural(got_ref, 32, 12, 0, 8), solver)
    solved_ref[...] = solved
    raw_ref[...] = gram(solved) * (1.0 / ROWS)
    own = some_rows(solved_ref, slot[0], BI)
    sums = [jnp.zeros((BJ, RANK), F32) for _ in range(2)]
    for n in range(BI):
        sums[n % 2] = sums[n % 2] + own[n : n + 1, :] * y_ref[n]
    partial_ref[...] = sums[0] + sums[1]
    core = lax.axis_index("ic")
    for ref, half in ((keep_ref, core), (send_ref, 1 - core)):
        ref[0:32, :] = some_rows(partial_ref, half, 32)
        ref[32:96, :] = some_rows(raw_ref, half, 64)
        ref[96:104, :] = jnp.full((8, RANK), slot[1].astype(F32))


def merge_kernel(keep_ref, other_ref, parts_ref):
    first = lax.broadcasted_iota(jnp.int32, (8, RANK), 0) == 0
    parts_ref[0:32, :] = keep_ref[0:32, :]
    parts_ref[32:64, :] = other_ref[0:32, :]
    parts_ref[64:72, :] = jnp.where(first, keep_ref[96:104, :], other_ref[96:104, :])
    parts_ref[72:136, :] = keep_ref[32:96, :] + other_ref[32:96, :]


def in_source_order(axis, refs, all_ref):
    size = refs[0].shape[0]
    me = lax.axis_index(axis)
    for step, ref in enumerate(refs):
        source = lax.rem(me + 4 - step, 4)
        all_ref[pl.ds(pl.multiple_of(source * size, 8), size), :] = ref[...]


def dense_kernel(parts_0, parts_1, parts_2, parts_3, half_ref, gram_ref, all_ref):
    in_source_order("iy", (parts_0, parts_1, parts_2, parts_3), all_ref)
    sums = [jnp.zeros((32, RANK), F32) for _ in range(SLOTS)]
    for n in range(4):
        for part in range(2):
            rows = all_ref[136 * n + 32 * part : 136 * n + 32 * part + 32, :]
            ids = all_ref[136 * n + 64 + part : 136 * n + 65 + part, :]
            for slot in range(SLOTS):
                sums[slot] = sums[slot] + jnp.where(ids == slot, rows, 0.0)
    for slot in range(SLOTS):
        half_ref[32 * slot : 32 * slot + 32, :] = sums[slot]
    grams = [all_ref[136 * n + 72 : 136 * n + 136, :] for n in range(4)]
    gram_ref[...] = (grams[0] + grams[1]) + (grams[2] + grams[3])


def sum_kernel(half_0, half_1, half_2, half_3, sum_ref, all_ref):
    in_source_order("ka", (half_0, half_1, half_2, half_3), all_ref)
    parts = [all_ref[RANK * n : RANK * n + RANK, :] for n in range(4)]
    sum_ref[...] = (parts[0] + parts[1]) + (parts[2] + parts[3])


def second_inverse_kernel(
    same_ref, other_ref, gram_c_ref, solved_a_ref,
    solver_ref, gram_a_ref, scale_ref, loading_a_ref, raw_ref,
):
    core = lax.axis_index("ic")
    for ref, half in ((same_ref, core), (other_ref, 1 - core)):
        raw_ref[pl.ds(pl.multiple_of(64 * half, 64), 64), :] = ref[...]
    scale, gram_a = scaled_gram(raw_ref[...])
    gram_a_ref[...] = gram_a
    scale_ref[...] = jnp.broadcast_to(scale, (8, RANK))
    loading_a_ref[...] = solved_a_ref[...] * scale
    solver_ref[...] = system_inverse(gram_a * gram_c_ref[...])


def third_kernel(
    coords_ref, same_ref, other_ref, solver_ref, scale_ref, solved_a_ref, block_ref,
    solved_ref, chunk_ref, khatri_ref, rows_ref,
):
    at, slot = places(coords_ref)
    core = lax.axis_index("ic")
    for ref, half in ((same_ref, core), (other_ref, 1 - core)):
        for n in range(SLOTS):
            place = pl.multiple_of(64 * n + 32 * half, 32)
            rows_ref[pl.ds(place, 32), :] = ref[32 * n : 32 * n + 32, :]
    solved_ref[...] = exact_dot(rows_ref[...] * scale_ref[0:1, :], solver_ref[...])
    raw = gram(some_rows(solved_ref, at[0], 32)) * (1.0 / ROWS)
    own_a = some_rows(solved_a_ref, slot[0], BI) * scale_ref[0:1, :]
    own_b = some_rows(solved_ref, slot[1], BJ)
    for n in range(BI):
        khatri_ref[n * BJ : (n + 1) * BJ, :] = (own_a[n : n + 1, :] * own_b).astype(BF16)
    partial = lax.dot_general(
        block_ref[...].reshape(BI * BJ, BK),
        khatri_ref[...],
        (((0,), (0,)), ((), ())),
        preferred_element_type=F32,
    )
    for t in range(2):
        put(chunk_ref, t, 64, 4, partial[64 * t : 64 * t + 64])
    put(chunk_ref, 2, 64, 4, raw[0:64])
    put(chunk_ref, 3, 64, 4, mark(raw[64:128], slot[2]))


def fourth_kernel(
    same_ref, other_ref, gram_a_ref, solved_b_ref, loading_b_ref, solved_ref, squares_ref, rows_ref
):
    core = lax.axis_index("ic")
    for ref, half in ((same_ref, core), (other_ref, 1 - core)):
        for t in range(10):
            for n in range(4):
                place = pl.multiple_of(64 * t + 16 * n + 8 * half, 8)
                rows_ref[pl.ds(place, 8), :] = strided(ref, 80 * n + t, 8, 10)
    scale, gram_b = scaled_gram(unmark(rows_ref[512:640, :]))
    loading_b_ref[...] = solved_b_ref[...] * scale
    solver = system_inverse(gram_a_ref[...] * gram_b)
    solved = exact_dot(rows_ref[0:512, :] * scale, solver)
    solved_ref[...] = solved
    squares_ref[...] = jnp.sum(solved * solved, axis=0, keepdims=True)


def call(kernel, operands, outs, scalars=0, scratch=(), space=pltpu.VMEM):
    vmem = pl.BlockSpec(memory_space=pltpu.VMEM)
    smem = pl.BlockSpec(memory_space=pltpu.SMEM)
    return pl.pallas_call(
        kernel,
        out_shape=[jax.ShapeDtypeStruct(shape, F32) for shape in outs],
        in_specs=[smem] * scalars + [pl.BlockSpec(memory_space=space)] * (len(operands) - scalars),
        out_specs=[vmem] * len(outs),
        scratch_shapes=scratch,
        compiler_params=pltpu.CompilerParams(vmem_limit_bytes=32 << 20),
    )(*operands)


def exchange(values, axes, *chunk):
    shape = values.shape
    return lax.all_to_all(values.reshape(chunk), axes, 0, 0, tiled=True).reshape(shape)


def swap_cores(values):
    return lax.ppermute(values, "ic", [(0, 1), (1, 0)])


def around(axis, values):
    return [
        lax.ppermute(values, axis, [(n, (n + step) % 4) for n in range(4)]) for step in (1, 2, 3)
    ]


def on_device(blocks, coords, live, factor_b, factor_c):
    block = blocks[0]
    coords = coords.reshape(3)
    full = (RANK, RANK)

    chunk, y = call(
        first_kernel,
        [pltpu.with_memory_space_constraint(v, pltpu.HBM) for v in (coords, block, factor_b, factor_c)],
        [(256, RANK), (BI, BJ, RANK)],
        0,
        [
            pltpu.VMEM((BI, BJ, BK), BF16),
            pltpu.VMEM((512, RANK), F32),
            pltpu.VMEM((256, RANK), F32),
            pltpu.SMEM((3,), jnp.int32),
            pltpu.SemaphoreType.DMA((7,)),
        ],
        pltpu.HBM,
    )
    got = exchange(chunk, ("ja", "ka"), 32, 8, RANK)
    spread, diagonal = call(collect_first_kernel, (got,), [(384, RANK), (8, RANK)])
    got = exchange(spread, ("ja", "ka"), 32, 3, 4, RANK)

    solved_a, gram_c, keep, send = call(
        second_kernel,
        (coords, got, diagonal, y),
        [(256, RANK), full, (104, RANK), (104, RANK)],
        1,
        [pltpu.VMEM((BJ, RANK), F32), pltpu.VMEM(full, F32)],
    )
    (parts,) = call(merge_kernel, (keep, swap_cores(send)), [(136, RANK)])
    half, gram_half = call(
        dense_kernel,
        (parts, *around("iy", parts)),
        [full, (64, RANK)],
        0,
        [pltpu.VMEM((544, RANK), F32)],
    )
    other = swap_cores(gram_half)
    around_x = around("ka", half)
    solver, gram_a, scale, loading_a = call(
        second_inverse_kernel,
        (gram_half, other, gram_c, solved_a),
        [full, full, (8, RANK), (256, RANK)],
        0,
        [pltpu.VMEM(full, F32)],
    )
    (half,) = call(sum_kernel, (half, *around_x), [full], 0, [pltpu.VMEM((512, RANK), F32)])

    solved_b, chunk = call(
        third_kernel,
        (coords, half, swap_cores(half), solver, scale, solved_a, block),
        [(256, RANK), (256, RANK)],
        1,
        [pltpu.VMEM((BI * BJ, RANK), BF16), pltpu.VMEM((256, RANK), F32)],
    )
    got = exchange(chunk, (*IA, "ja"), 64, 4, RANK)
    (spread,) = call(collect_third_kernel, (got,), [(320, RANK)])
    same = exchange(spread, ("iy", "ja"), 32, 5, 2, RANK)
    other = swap_cores(same)

    loading_b, solved_c, squares = call(
        fourth_kernel,
        (same, other, gram_a, solved_b),
        [(256, RANK), (512, RANK), (1, RANK)],
        0,
        [pltpu.VMEM((640, RANK), F32)],
    )
    total = squares + sum(around("ka", squares))
    loading_c = solved_c * lax.rsqrt(total / ROWS + EPSILON)
    return (loading_a, loading_b, loading_c)


def solution(mesh):
    shape = mesh.devices.shape
    split = jax.sharding.Mesh(
        mesh.devices.reshape(shape[0] // 2, 2, *shape[1:]), (*IA, "ja", "ka")
    )
    every = (*IA, "ja", "ka")
    placed = (P(every, None, None, None), P(None, every), P(every), P("ja", None), P("ka", None))
    return jax.shard_map(
        on_device,
        mesh=split,
        in_specs=placed,
        out_specs=(P(IA, None), P("ja", None), P("ka", None)),
        check_vma=False,
    )
```
